256 devices in a mesh: members: 16 (over z_hi, y, core), lat: 4 (over x), blk: 4 (over z_lo).
Axes of the slice: x: 4, y: 4, z: 8 (z_hi: 2, z_lo: 4; z = z_hi * 4 + z_lo), core: 2. Of those that a mesh axis runs over, the one named last changes fastest.
Arguments:
- starting_states: float32 [512, 256, 768], P(('members', 'blk'), 'lat'), may hold values from -6 to 6
- courant_x: float32 [256, 768], P('lat'), may hold values from -0.3 to 0.3
- courant_y: float32 [256, 768], P('lat'), may hold values from -0.3 to 0.3
- diffusion: float32 [256, 768], P('lat'), may hold values from 0.05 to 0.2
- obs_index: int32 [4, 64, 128], P('lat', ('members', 'blk')), may hold values from 0 to 767
- obs_value: float32 [4, 64, 128], P('lat', ('members', 'blk')), may hold values from -6 to 6
- loc_weight: float32 [4, 64, 3, 128], P('lat', ('members', 'blk')), may hold values from 0.1 to 1
Outputs:
- analysis: float32 [512, 256, 768], P(('members', 'blk'), 'lat')
The draws below stay inside these ranges and needn't reach their ends.
Inputs may be any that keep to these rules, and one draw needn't show every extreme that they name: `obs_index`: positions among the 768 cells of the block, counted row by row; repeats may occur.
All inputs are finite; a program needn't handle non-finite values.
Results may differ from the reference program's by a relative error of at most 0.0003.
Values sent between devices are 32-bit elements; how exact they have to be, the bound alone decides.
A program may use at most 64 MiB of HBM per device.

```python
import math
import jax
import jax.numpy as jnp
from jax import lax

MEMBERS = 512
NLON = 768
OBS = 128
FSTEPS = 8
NS_ITERS = 4
NLAT = 256
CELLS_BLK = 768
SUBS = 64
N_LAT = 4


def place_ends(values, stream_key, smallest, top_value):
    index_at = [jax.random.randint(jax.random.fold_in(stream_key, axis), (), 0, length) for axis, length in enumerate(values.shape)]
    widest = values.shape.index(max(values.shape))
    next_to = index_at[:widest] + [(index_at[widest] + 1) % values.shape[widest]] + index_at[widest + 1:]
    return values.at[tuple(index_at)].set(smallest).at[tuple(next_to)].set(top_value)


def steps_of(rng, shape, cuts, smallest, high):
    def one(position, blocks):
        steps = jax.random.uniform(jax.random.fold_in(jax.random.fold_in(rng, 6), position), (blocks,), jnp.float32, smallest / len(cuts), high / len(cuts))
        return jnp.repeat(jnp.exp(steps), shape[position] // blocks).reshape((-1,) + (1,) * (len(shape) - position - 1))

    loudness = one(*cuts[0])
    for cut in cuts[1:]:
        loudness = loudness * one(*cut)
    return loudness


def bell_draw(rng, shape, width, limit, cuts=(), kind=jnp.bfloat16):
    entries = width * jax.random.normal(rng, shape, jnp.float32)
    if cuts:
        entries = entries * steps_of(rng, shape, cuts, -0.22, 0.18)
    return jnp.clip(entries, -limit, limit).astype(kind)


def setup_inputs(seed: int = 0) -> dict:
    splits = jax.random.split(jax.random.key(seed), 8)
    starting_states = bell_draw(splits[0], (MEMBERS, NLAT, NLON), 1.0, 6.0, ((0, 64), (1, 4)), jnp.float32)
    courant_x = jnp.clip(jax.random.uniform(splits[1], (NLAT, NLON), jnp.float32, -0.3, 0.3) * steps_of(splits[1], (NLAT, NLON), ((0, 4),), -0.4, 0.0), -0.3, 0.3)
    courant_y = jnp.clip(jax.random.uniform(splits[2], (NLAT, NLON), jnp.float32, -0.3, 0.3) * steps_of(splits[2], (NLAT, NLON), ((0, 4),), -0.4, 0.0), -0.3, 0.3)
    diffusion = jnp.clip(0.05 + 0.15 * jax.random.uniform(splits[3], (NLAT, NLON), jnp.float32) ** steps_of(splits[3], (NLAT, NLON), ((0, 4),), -0.2, 0.2), 0.05, 0.2)
    obs_index = place_ends(jax.random.randint(splits[4], (N_LAT, SUBS, OBS), 0, CELLS_BLK), jax.random.fold_in(splits[4], 1), 0, CELLS_BLK - 1).astype(jnp.int32)
    obs_value = bell_draw(splits[5], (N_LAT, SUBS, OBS), 1.0, 6.0, ((0, 4), (1, 64)), jnp.float32)
    loc_weight = jnp.clip(jnp.exp(math.log(1.0) - 2.3025851 * jax.random.uniform(splits[6], (N_LAT, SUBS, 3, OBS), jnp.float32) ** steps_of(splits[6], (N_LAT, SUBS, 3, OBS), ((0, 4), (1, 64)), -0.2, 0.2)), 0.1, 1.0)
    return dict(starting_states=starting_states, courant_x=courant_x, courant_y=courant_y, diffusion=diffusion, obs_index=obs_index, obs_value=obs_value, loc_weight=loc_weight)


HIGH = lax.Precision.HIGHEST

def advance(field_now, courant_x, courant_y, diffusion):
    zero_row = jnp.zeros((1, field_now.shape[1]), jnp.float32)
    row_above = jnp.concatenate([field_now[1:], zero_row], axis=0)
    row_below = jnp.concatenate([zero_row, field_now[:-1]], axis=0)
    eastward_column = jnp.roll(field_now, -1, axis=1)
    col_west = jnp.roll(field_now, 1, axis=1)
    return field_now + 0.5 * courant_x * (col_west - eastward_column) + 0.5 * courant_y * (row_below - row_above) + diffusion * (eastward_column + col_west + row_above + row_below - 4.0 * field_now)

def transform(block, stacked_members, innovation, weights):
    realization_number = block.shape[0]
    centre = lax.optimization_barrier(jnp.mean(block, axis=0))
    anomaly = block - centre
    weighted = stacked_members * weights
    identity = jnp.eye(realization_number, dtype=jnp.float32)
    gram = identity + jnp.dot(weighted, stacked_members.T, precision=HIGH) / (realization_number - 1)
    frobenius = jnp.sqrt(jnp.sum(gram * gram) + 1e-06)
    iterate = gram / frobenius
    inverse = identity
    for repeat in range(NS_ITERS):
        factor = 1.5 * identity - 0.5 * jnp.dot(inverse, iterate, precision=HIGH)
        iterate = jnp.dot(iterate, factor, precision=HIGH)
        inverse = jnp.dot(factor, inverse, precision=HIGH)
    inv_root = inverse / jnp.sqrt(frobenius)
    pull_term = jnp.dot(weighted, innovation, precision=HIGH)
    shift_mean = jnp.dot(inv_root, jnp.dot(inv_root, pull_term, precision=HIGH), precision=HIGH) / (realization_number - 1)
    mixing = inv_root + shift_mean[:, None]
    return centre[None, :] + jnp.dot(mixing.T, anomaly, precision=HIGH)

def reference(starting_states, courant_x, courant_y, diffusion, obs_index, obs_value, loc_weight):

    def prognosis_surface(realization_thickness):
        for repeat in range(FSTEPS):
            realization_thickness = advance(realization_thickness, courant_x, courant_y, diffusion)
        return realization_thickness
    projected_thickness = lax.map(prognosis_surface, starting_states)
    block_count = N_LAT * SUBS
    blocks = jnp.transpose(projected_thickness.reshape(MEMBERS, block_count, CELLS_BLK), (1, 0, 2))
    positions = obs_index.reshape(block_count, OBS)
    observed = obs_value.reshape(block_count, OBS)
    weight_rows = loc_weight.reshape(block_count, 3 * OBS)

    def observe(packed_values):
        block, cells, values = packed_values
        ybank = jnp.take(block, cells, axis=1)
        ybar = lax.optimization_barrier(jnp.mean(ybank, axis=0))
        return (ybank - ybar, values - ybar)
    own_anom, local_innovation = lax.map(observe, (blocks, positions, observed))
    strips_anom = own_anom.reshape(N_LAT, SUBS, MEMBERS, OBS)
    strips_innov = local_innovation.reshape(N_LAT, SUBS, OBS)
    zero_anom = jnp.zeros((N_LAT, 1, MEMBERS, OBS), jnp.float32)
    zero_innov = jnp.zeros((N_LAT, 1, OBS), jnp.float32)
    prev_anom = jnp.concatenate([zero_anom, strips_anom[:, :-1]], axis=1).reshape(block_count, MEMBERS, OBS)
    next_anom = jnp.concatenate([strips_anom[:, 1:], zero_anom], axis=1).reshape(block_count, MEMBERS, OBS)
    prev_innov = jnp.concatenate([zero_innov, strips_innov[:, :-1]], axis=1).reshape(block_count, OBS)
    next_innovation = jnp.concatenate([strips_innov[:, 1:], zero_innov], axis=1).reshape(block_count, OBS)

    def analyse(packed_values):
        block, anom_prev, anom_own, anom_next, innov_prev, innov_own, innov_next, weights = packed_values
        stacked_members = jnp.concatenate([anom_prev, anom_own, anom_next], axis=1)
        innovation = jnp.concatenate([innov_prev, innov_own, innov_next], axis=0)
        return transform(block, stacked_members, innovation, weights)
    corrected_states = lax.map(analyse, (blocks, prev_anom, own_anom, next_anom, prev_innov, local_innovation, next_innovation, weight_rows))
    return jnp.transpose(corrected_states, (1, 0, 2)).reshape(MEMBERS, NLAT, NLON)
```

```python
import functools

import jax
import jax.numpy as jnp
from jax import lax
from jax.experimental import pallas as pl
from jax.experimental.pallas import tpu as pltpu
from jax.sharding import PartitionSpec as P

FSTEPS = 8
NS_ITERS = 4
ROWS = 16
AHEAD = 16
MESH = pl.DeviceIdType.MESH
VMEM = pl.BlockSpec(memory_space=pltpu.VMEM)
F32 = jnp.float32
BF16 = jnp.bfloat16


def split(x):
    high = x.astype(BF16)
    return high, (x - high.astype(F32)).astype(BF16)


def dot3(a, b, contract=((1,), (0,))):
    def one(p, q):
        return lax.dot_general(p, q, (contract, ((), ())), preferred_element_type=F32)

    return one(a[0], b[0]) + (one(a[0], b[1]) + one(a[1], b[0]))


def whole_kernel(
    state_ref, cx_ref, cy_ref, d_ref, index_ref, terms_ref, out_ref,
    levels, dense, coef, cells, obs, terms, block, seen, stack, result,
    gram, left_hi, left_lo, right_hi, right_lo, inv_hi, inv_lo, wide_hi, wide_lo, anom_hi, anom_lo,
    load_sem, coef_sem, send_sem, edge_send, edge_recv, cell_sem, term_sem, obs_sem, field_sem, low_sem, high_sem, back_sem,
):
    per, count, lon = state_ref.shape
    members = count * per
    tall = count + 2 * FSTEPS
    lo = lax.axis_index("members")
    bl = lax.axis_index("blk")
    lat = lax.axis_index("lat")
    n_lat = lax.axis_size("lat")
    n_blk = lax.axis_size("blk")
    me = lo * n_blk + bl
    my_z, my_y, my_core = (lo // 8) * 4 + bl, (lo // 2) % 4, lo % 2

    def set_at(z, y, core):
        return (((z // 4) * 4 + y) * 2 + core) * 4 + z % 4

    def block_at(z, y, core):
        return (z * 4 + y + (z % 2) * (3 - 2 * y)) * 2 + core

    def own_of(b):
        z, y = b // 8, (b // 2) % 4
        return set_at(z, y + (z % 2) * (3 - 2 * y), b % 2)

    def place(k):
        return {"members": k // n_blk, "blk": k % n_blk}

    def peer_of(t):
        dz, dcore, dy = t % 8, (t // 8) % 2, t // 16
        at = (my_z + dz) % 8, (my_y + dy) % 4, (my_core + dcore) % 2
        return set_at(*at), block_at(*at)

    mine = block_at(my_z, my_y, my_core)
    my_rows = pl.ds(pl.multiple_of(me * per, per), per)
    inner = pl.ds(FSTEPS, count)

    for m in range(per):
        pltpu.make_async_copy(state_ref.at[m], levels.at[inner, m, :], load_sem).start()

    barrier = pltpu.get_barrier_semaphore()

    def greet(t, carry):
        k, _ = peer_of(t)
        pl.semaphore_signal(barrier, inc=1, device_id=place(k), device_id_type=MESH)
        return carry

    @pl.when(lat > 0)
    def _():
        pl.semaphore_signal(barrier, inc=1, device_id={"lat": lat - 1}, device_id_type=MESH)

    @pl.when(lat < n_lat - 1)
    def _():
        pl.semaphore_signal(barrier, inc=1, device_id={"lat": lat + 1}, device_id_type=MESH)

    lax.fori_loop(1, count, greet, 0)

    cx, cy, d = 0.5 * cx_ref[...], 0.5 * cy_ref[...], d_ref[...]
    for i, value in enumerate((1.0 - 4.0 * d, d - cx, d + cx, d - cy, d + cy)):
        dense[i] = value
        pltpu.make_async_copy(dense.at[i], coef.at[inner, i, :], coef_sem).start()
    cells[me] = index_ref[0]
    low_rows, high_rows = pl.ds(0, FSTEPS), pl.ds(FSTEPS + count, FSTEPS)

    @pl.when(lat == 0)
    def _():
        levels[low_rows] = jnp.zeros((FSTEPS, per, lon), F32)
        coef[low_rows] = jnp.zeros((FSTEPS, per, lon), F32)

    @pl.when(lat == n_lat - 1)
    def _():
        levels[high_rows] = jnp.zeros((FSTEPS, per, lon), F32)
        coef[high_rows] = jnp.zeros((FSTEPS, per, lon), F32)

    pltpu.make_async_copy(levels.at[inner], levels.at[inner], load_sem).wait()
    pltpu.make_async_copy(dense, dense, coef_sem).wait()
    pl.semaphore_wait(
        barrier, count - 1 + jnp.where(lat > 0, 1, 0) + jnp.where(lat < n_lat - 1, 1, 0)
    )

    def edges(up):
        source = pl.ds(count if up else FSTEPS, FSTEPS)
        target = low_rows if up else high_rows
        side = 0 if up else 1
        device = {"lat": lat + 1 if up else lat - 1}
        return [
            pltpu.make_async_remote_copy(
                levels.at[source], levels.at[target], edge_send.at[side, 0], edge_recv.at[side, 0],
                device_id=device, device_id_type=MESH,
            ),
            pltpu.make_async_remote_copy(
                coef.at[source], coef.at[target], edge_send.at[side, 1],
                edge_recv.at[side, 1], device_id=device, device_id_type=MESH,
            ),
        ]

    @pl.when(lat < n_lat - 1)
    def _():
        for copy in edges(True):
            copy.start()

    @pl.when(lat > 0)
    def _():
        for copy in edges(False):
            copy.start()

    def send_cells(t, carry):
        k, _ = peer_of(t)
        pltpu.make_async_remote_copy(
            index_ref.at[0], cells.at[me], send_sem.at[5], cell_sem,
            device_id=place(k), device_id_type=MESH,
        ).start()
        return carry

    lax.fori_loop(1, count, send_cells, 0)

    def send_terms():
        return pltpu.make_async_remote_copy(
            terms_ref, terms, send_sem.at[6], term_sem,
            device_id=place(own_of(me)), device_id_type=MESH,
        )

    @pl.when(mine == me)
    def _():
        terms[...] = terms_ref[...]

    @pl.when(mine != me)
    def _():
        send_terms().start()

    lane = lax.broadcasted_iota(jnp.int32, (per, 128), 1)
    parts = lon // 128

    def advance_row(step, r):
        now = (step - 1) * tall + r
        pieces = [levels[now, :, p * 128 : (p + 1) * 128] for p in range(parts)]
        right = [pltpu.roll(v, 1, 1) for v in pieces]
        left = [pltpu.roll(v, 127, 1) for v in pieces]
        for p in range(parts):
            here = slice(p * 128, (p + 1) * 128)
            west = jnp.where(lane == 0, right[p - 1], right[p])
            east = jnp.where(lane == 127, left[(p + 1) % parts], left[p])
            c = [jnp.broadcast_to(coef[r, pl.ds(i, 1), here], lane.shape) for i in range(5)]
            levels[now + tall, :, here] = (
                (c[0] * pieces[p] + c[1] * east)
                + (c[2] * west + c[3] * levels[now + 1, :, here])
                + c[4] * levels[now - 1, :, here]
            )

    def inner_step(step, carry):
        low, high = FSTEPS + step, FSTEPS + count - step

        def rows(i, inner_carry):
            start = jnp.minimum(low + ROWS * i, high - ROWS)
            for u in range(ROWS):
                advance_row(step, start + u)
            return inner_carry

        return lax.fori_loop(0, (high - low + ROWS - 1) // ROWS, rows, carry)

    lax.fori_loop(1, FSTEPS + 1, inner_step, 0)

    @pl.when(lat > 0)
    def _():
        for copy in edges(True):
            copy.wait_recv()
        for copy in edges(False):
            copy.wait_send()

    @pl.when(lat < n_lat - 1)
    def _():
        for copy in edges(False):
            copy.wait_recv()
        for copy in edges(True):
            copy.wait_send()

    def edge_step(step, carry):
        for u in range(FSTEPS):
            advance_row(step, step + u)
            advance_row(step, tall - step - FSTEPS + u)
        return carry

    lax.fori_loop(1, FSTEPS + 1, edge_step, 0)
    final = FSTEPS * tall + FSTEPS

    pltpu.make_async_copy(cells.at[: count - 1], cells.at[: count - 1], cell_sem).wait()

    def observe(i, carry):
        for u in range(8):
            k = i * 8 + u
            b = k
            index = jnp.broadcast_to(cells[k], lane.shape)
            where, group = jnp.bitwise_and(index, 127), jnp.right_shift(index, 7)
            found = jnp.zeros(lane.shape, F32)
            for p in range(parts):
                picked = jnp.take_along_axis(
                    levels[final + b, :, p * 128 : (p + 1) * 128], where, axis=1
                )
                found = jnp.where(group == p, picked, found)
            obs[b] = found
        return carry

    lax.fori_loop(0, count // 8, observe, 0)

    def send_obs(t, carry):
        k, b = peer_of(t)
        pltpu.make_async_remote_copy(
            obs.at[b], seen.at[my_rows, :], send_sem.at[0], obs_sem,
            device_id=place(k), device_id_type=MESH,
        ).start()
        return carry

    def send_field(t, carry):
        k, b = peer_of(t)
        pltpu.make_async_remote_copy(
            levels.at[final + b], block.at[my_rows, :], send_sem.at[1], field_sem,
            device_id=place(k), device_id_type=MESH,
        ).start()
        return carry

    lax.fori_loop(1, count, send_obs, 0)
    lax.fori_loop(1, AHEAD, send_field, 0)
    seen[my_rows, :] = obs[mine]
    block[my_rows, :] = levels[final + mine]

    @pl.when(mine != me)
    def _():
        send_terms().wait()

    others = (count - 1) * per
    pltpu.make_async_copy(seen.at[:others], seen.at[:others], obs_sem).wait()

    ybar = jnp.mean(seen[...], axis=0, keepdims=True)
    own = seen[...] - ybar
    stack[1, :members, :] = own
    stack[1, members:, :] = jnp.broadcast_to(terms[pl.ds(0, 1), :] - ybar, (8, own.shape[1]))

    def to_low():
        return pltpu.make_async_remote_copy(
            stack.at[1], stack.at[2], send_sem.at[2], high_sem,
            device_id=place(own_of(mine - 1)), device_id_type=MESH,
        )

    def to_high():
        return pltpu.make_async_remote_copy(
            stack.at[1], stack.at[0], send_sem.at[3], low_sem,
            device_id=place(own_of(mine + 1)), device_id_type=MESH,
        )

    @pl.when(mine > 0)
    def _():
        to_low().start()

    @pl.when(mine < count - 1)
    def _():
        to_high().start()

    lax.fori_loop(AHEAD, count, send_field, 0)

    @pl.when(mine == 0)
    def _():
        stack[0] = jnp.zeros(stack.shape[1:], F32)

    @pl.when(mine == count - 1)
    def _():
        stack[2] = jnp.zeros(stack.shape[1:], F32)

    @pl.when(mine > 0)
    def _():
        to_low().wait_send()
        to_high().wait_recv()

    @pl.when(mine < count - 1)
    def _():
        to_high().wait_send()
        to_low().wait_recv()

    obs = own.shape[1]
    pull = jnp.zeros((members, 1), F32)
    for part in range(3):
        held = stack[part, :members, :]
        weighted = held * terms[pl.ds(1 + part, 1), :]
        pull = pull + jnp.sum(weighted * stack[part, pl.ds(members, 1), :], axis=1, keepdims=True)
        here = slice(part * obs, (part + 1) * obs)
        wide_hi[:, here], wide_lo[:, here] = split(held)
        left_hi[:, here], left_lo[:, here] = split(weighted)

    rows = 128
    chunks = members // rows

    def eye(start):
        row = lax.broadcasted_iota(jnp.int32, (rows, members), 0) + start
        return (row == lax.broadcasted_iota(jnp.int32, (rows, members), 1)).astype(F32)

    def at(i):
        return pl.ds(pl.multiple_of(i * rows, rows), rows)

    width = 3 * obs

    def gram_rows(i, total):
        part = dot3(
            (left_hi[at(i), :width], left_lo[at(i), :width]),
            (wide_hi[...], wide_lo[...]), ((1,), (1,)),
        )
        part = part / (members - 1) + eye(i * rows)
        gram[at(i), :] = part
        return total + jnp.sum(part * part, keepdims=True)

    total = lax.fori_loop(0, chunks, gram_rows, jnp.zeros((1, 1), F32))
    frobenius = jnp.sqrt(total + 1e-06)

    def scale_rows(i, carry):
        gram[at(i), :] = gram[at(i), :] / frobenius
        return carry

    lax.fori_loop(0, chunks, scale_rows, 0)

    for repeat in range(NS_ITERS):
        last = repeat == NS_ITERS - 1

        def factor_rows(i, carry, repeat=repeat):
            now = gram[at(i), :]
            right_hi[at(i), :], right_lo[at(i), :] = split(1.5 * eye(i * rows) - 0.5 * now)
            left_hi[at(i), :], left_lo[at(i), :] = split(now)
            if repeat == 0:
                inv_hi[at(i), :], inv_lo[at(i), :] = right_hi[at(i), :], right_lo[at(i), :]
            return carry

        lax.fori_loop(0, chunks, factor_rows, 0)

        def step_rows(i, carry, repeat=repeat, last=last):
            right = (right_hi[...], right_lo[...])
            if not last:
                half = dot3((left_hi[at(i), :], left_lo[at(i), :]), right)
                gram[at(i), :] = dot3(split(half), right)
            if repeat > 0:
                inverse = dot3((inv_hi[at(i), :], inv_lo[at(i), :]), right)
                if last:
                    gram[at(i), :] = inverse / jnp.sqrt(frobenius)
                else:
                    inv_hi[at(i), :], inv_lo[at(i), :] = split(inverse)
            return carry

        lax.fori_loop(0, chunks, step_rows, 0)

    inner = jnp.sum(gram[...] * pull, axis=0, keepdims=True)
    shift = jnp.sum(gram[...] * inner, axis=1, keepdims=True) / (members - 1)

    def cut_rows(i, carry):
        inv_hi[at(i), :], inv_lo[at(i), :] = split(gram[at(i), :])
        return carry

    lax.fori_loop(0, chunks, cut_rows, 0)

    pltpu.make_async_copy(block.at[:others], block.at[:others], field_sem).wait()
    centre = jnp.mean(block[...], axis=0, keepdims=True)
    anomaly = block[...] - centre
    anom_hi[...], anom_lo[...] = split(anomaly)
    base = centre + jnp.sum(anomaly * shift, axis=0, keepdims=True)

    group = rows // per

    def back(k):
        return pltpu.make_async_remote_copy(
            result.at[pl.ds(pl.multiple_of(k * per, per), per), :], out_ref.at[mine],
            send_sem.at[4], back_sem, device_id=place(k), device_id_type=MESH,
        )

    def final_rows(i, carry):
        c = (me // group + i) % chunks
        result[at(c), :] = base + dot3(
            (inv_hi[at(c), :], inv_lo[at(c), :]), (anom_hi[...], anom_lo[...])
        )

        def send(j, inner_carry):
            k = c * group + (me + j) % group

            @pl.when(k != me)
            def _():
                back(k).start()

            return inner_carry

        return lax.fori_loop(0, group, send, carry)

    lax.fori_loop(0, chunks, final_rows, 0)
    out_ref[mine] = result[my_rows, :]

    pltpu.make_async_copy(out_ref.at[: count - 1], out_ref.at[: count - 1], back_sem).wait()
    pltpu.make_async_copy(seen.at[:others], seen.at[:others], send_sem.at[0]).wait()
    pltpu.make_async_copy(block.at[:others], block.at[:others], send_sem.at[1]).wait()
    pltpu.make_async_copy(block.at[:others], block.at[:others], send_sem.at[4]).wait()
    pltpu.make_async_copy(cells.at[: count - 1], cells.at[: count - 1], send_sem.at[5]).wait()


def whole(state, cx, cy, d, index, terms):
    per, count, lon = state.shape
    members, width = count * per, terms.shape[1]
    tall = count + 2 * FSTEPS
    square = (members, members)
    return pl.pallas_call(
        whole_kernel,
        out_shape=jax.ShapeDtypeStruct((count, per, lon), F32),
        in_specs=[pl.BlockSpec(memory_space=pl.ANY)] + [VMEM] * 5,
        out_specs=VMEM,
        scratch_shapes=[
            pltpu.VMEM(((FSTEPS + 1) * tall, per, lon), F32),
            pltpu.VMEM((5, count, lon), F32),
            pltpu.VMEM((tall, per, lon), F32),
            pltpu.VMEM((count, 1, width), jnp.int32),
            pltpu.VMEM((count, per, width), F32),
            pltpu.VMEM(terms.shape, F32),
            pltpu.VMEM((members, lon), F32),
            pltpu.VMEM((members, width), F32),
            pltpu.VMEM((3, members + 8, width), F32),
            pltpu.VMEM((members, lon), F32),
            pltpu.VMEM(square, F32),
        ]
        + [pltpu.VMEM(square, BF16)] * 6
        + [pltpu.VMEM((members, 3 * width), BF16)] * 2
        + [pltpu.VMEM((members, lon), BF16)] * 2
        + [
            pltpu.SemaphoreType.DMA,
            pltpu.SemaphoreType.DMA,
            pltpu.SemaphoreType.DMA((7,)),
            pltpu.SemaphoreType.DMA((2, 2)),
            pltpu.SemaphoreType.DMA((2, 2)),
        ]
        + [pltpu.SemaphoreType.DMA] * 7,
        compiler_params=pltpu.CompilerParams(
            collective_id=0, has_side_effects=True, vmem_limit_bytes=56 << 20
        ),
        cost_estimate=pl.CostEstimate(
            flops=10_000_000_000, bytes_accessed=6_000_000, transcendentals=0
        ),
    )(state, cx, cy, d, index, terms)


def on_device(starting_states, courant_x, courant_y, diffusion, obs_index, obs_value, loc_weight):
    terms = jnp.concatenate(
        [obs_value.reshape(1, -1), loc_weight.reshape(3, -1), jnp.zeros((4, obs_value.shape[2]), F32)]
    )
    out = whole(starting_states, courant_x, courant_y, diffusion, obs_index, terms)
    return jnp.transpose(out, (1, 0, 2))


def solution(mesh):
    in_specs = (
        P(("members", "blk"), "lat", None),
        P("lat", None),
        P("lat", None),
        P("lat", None),
        P("lat", ("members", "blk"), None),
        P("lat", ("members", "blk"), None),
        P("lat", ("members", "blk"), None, None),
    )
    out_specs = P(("members", "blk"), "lat", None)
    return jax.shard_map(
        on_device, mesh=mesh, in_specs=in_specs, out_specs=out_specs, check_vma=False
    )
```

```python
import functools

import jax
import jax.numpy as jnp
from jax import lax
from jax.experimental import pallas as pl
from jax.experimental.pallas import tpu as pltpu
from jax.sharding import PartitionSpec as P

FSTEPS = 8
NS_ITERS = 4
ROWS = 16
EARLY = 2
AHEAD = 4
ALONE = 3
SPIRAL = (1, 7, 2, 6, 3, 5, 4, 0)
MESH = pl.DeviceIdType.MESH
VMEM = pl.BlockSpec(memory_space=pltpu.VMEM)
F32 = jnp.float32
BF16 = jnp.bfloat16


def split(x):
    high = x.astype(BF16)
    return high, (x - high.astype(F32)).astype(BF16)


def dot3(a, b, contract=((1,), (0,))):
    def one(p, q):
        return lax.dot_general(p, q, (contract, ((), ())), preferred_element_type=F32)

    return one(a[0], b[0]) + (one(a[0], b[1]) + one(a[1], b[0]))


def whole_kernel(
    state_ref, cx_ref, cy_ref, d_ref, index_ref, value_ref, weight_ref, out_ref,
    l0, l1, l2, l3, l4, l5, l6, l7, l8,
    dense, coef, cells, obs, value, weight, block, seen, stack, result,
    spread_ref, gram, left_hi, left_lo, right_hi, right_lo, inv_hi, inv_lo, wide_hi, wide_lo, field_hi, field_lo,
    load_sem, coef_sem, send_sem, edge_send, edge_recv,
    cell_sem, value_sem, weight_sem, obs_sem, field_sem, low_sem, high_sem, back_sem,
):
    levels = (l0, l1, l2, l3, l4, l5, l6, l7, l8)
    per, count, lon = state_ref.shape
    members = count * per
    tall = count + 2 * FSTEPS
    lo = lax.axis_index("members")
    bl = lax.axis_index("blk")
    lat = lax.axis_index("lat")
    n_lat = lax.axis_size("lat")
    n_blk = lax.axis_size("blk")
    me = lo * n_blk + bl
    my_z, my_y, my_core = (lo // 8) * 4 + bl, (lo // 2) % 4, lo % 2

    def set_at(z, y, core):
        return (((z // 4) * 4 + y) * 2 + core) * 4 + z % 4

    def block_at(z, y, core):
        return (z * 4 + y + (z % 2) * (3 - 2 * y)) * 2 + core

    def own_of(b):
        z, y = b // 8, (b // 2) % 4
        return set_at(z, y + (z % 2) * (3 - 2 * y), b % 2)

    def place(k):
        return {"members": k // n_blk, "blk": k % n_blk}

    zs = [lax.rem(my_z + dz, 8) for dz in range(8)]
    z_sets = [lax.div(z, 4) * 8 for z in zs]
    z_blks = [lax.rem(z, 4) for z in zs]

    def each(first, last, act):
        def group(q, carry):
            y = lax.rem(my_y + lax.div(q, 2), 4)
            core = lax.rem(my_core + lax.rem(q, 2), 2)
            even, odd = y * 2 + core, (3 - y) * 2 + core
            for dz in SPIRAL:
                z = zs[dz]
                m, blk = z_sets[dz] + even, z_blks[dz]
                b = z * 8 + even + lax.rem(z, 2) * (odd - even)
                run = functools.partial(act, {"members": m, "blk": blk}, m * 4 + blk, b, z)
                if dz == 0:
                    pl.when(q > 0)(run)
                else:
                    run()
            return carry

        lax.fori_loop(first, last, group, 0)

    mine = block_at(my_z, my_y, my_core)
    my_rows = pl.ds(pl.multiple_of(me * per, per), per)
    inner = pl.ds(FSTEPS, count)

    for m in range(per):
        pltpu.make_async_copy(state_ref.at[m], l0.at[inner, m, :], load_sem).start()

    barrier = pltpu.get_barrier_semaphore()

    @pl.when(lat > 0)
    def _():
        pl.semaphore_signal(barrier, inc=1, device_id={"lat": lat - 1}, device_id_type=MESH)

    @pl.when(lat < n_lat - 1)
    def _():
        pl.semaphore_signal(barrier, inc=1, device_id={"lat": lat + 1}, device_id_type=MESH)

    def greet(device, k, b, z):
        pl.semaphore_signal(barrier, inc=1, device_id=device, device_id_type=MESH)

    each(0, 8, greet)

    cx, cy, d = 0.5 * cx_ref[...], 0.5 * cy_ref[...], d_ref[...]
    for i, term in enumerate((1.0 - 4.0 * d, d - cx, d + cx, d - cy, d + cy)):
        dense[i] = term
        pltpu.make_async_copy(dense.at[i], coef.at[inner, i, :], coef_sem).start()
    cells[me] = index_ref[0]
    low_rows, high_rows = pl.ds(0, FSTEPS), pl.ds(FSTEPS + count, FSTEPS)

    @pl.when(lat == 0)
    def _():
        l0[low_rows] = jnp.zeros((FSTEPS, per, lon), F32)
        coef[low_rows] = jnp.zeros((FSTEPS, per, lon), F32)

    @pl.when(lat == n_lat - 1)
    def _():
        l0[high_rows] = jnp.zeros((FSTEPS, per, lon), F32)
        coef[high_rows] = jnp.zeros((FSTEPS, per, lon), F32)

    lane = lax.broadcasted_iota(jnp.int32, (per, 128), 1)
    parts = lon // 128

    def advance_row(step, r):
        old, new = levels[step - 1], levels[step]
        pieces = [old[r, :, p * 128 : (p + 1) * 128] for p in range(parts)]
        right = [pltpu.roll(v, 1, 1) for v in pieces]
        left = [pltpu.roll(v, 127, 1) for v in pieces]
        for p in range(parts):
            here = slice(p * 128, (p + 1) * 128)
            west = jnp.where(lane == 0, right[p - 1], right[p])
            east = jnp.where(lane == 127, left[(p + 1) % parts], left[p])
            c = [jnp.broadcast_to(coef[r, pl.ds(i, 1), here], lane.shape) for i in range(5)]
            new[r, :, here] = (
                (c[0] * pieces[p] + c[1] * east)
                + (c[2] * west + c[3] * old[r + 1, :, here])
                + c[4] * old[r - 1, :, here]
            )

    def inner_step(step):
        low, high = FSTEPS + step, FSTEPS + count - step

        def rows(i, carry):
            start = jnp.minimum(low + ROWS * i, high - ROWS)
            for u in range(ROWS):
                advance_row(step, start + u)
            return carry

        lax.fori_loop(0, (high - low + ROWS - 1) // ROWS, rows, 0)

    pltpu.make_async_copy(l0.at[inner], l0.at[inner], load_sem).wait()
    pltpu.make_async_copy(dense, dense, coef_sem).wait()
    for step in range(1, ALONE + 1):
        inner_step(step)
    pl.semaphore_wait(
        barrier, count - 1 + jnp.where(lat > 0, 1, 0) + jnp.where(lat < n_lat - 1, 1, 0)
    )

    def edges(up):
        source = pl.ds(count if up else FSTEPS, FSTEPS)
        target = low_rows if up else high_rows
        side = 0 if up else 1
        device = {"lat": lat + 1 if up else lat - 1}
        return [
            pltpu.make_async_remote_copy(
                l0.at[source], l0.at[target], edge_send.at[side, 0], edge_recv.at[side, 0],
                device_id=device, device_id_type=MESH,
            ),
            pltpu.make_async_remote_copy(
                coef.at[source], coef.at[target], edge_send.at[side, 1],
                edge_recv.at[side, 1], device_id=device, device_id_type=MESH,
            ),
        ]

    @pl.when(lat < n_lat - 1)
    def _():
        for copy in edges(True):
            copy.start()

    @pl.when(lat > 0)
    def _():
        for copy in edges(False):
            copy.start()

    def send_cells(device, k, b, z):
        pltpu.make_async_remote_copy(
            index_ref.at[0], cells.at[me], send_sem.at[5], cell_sem,
            device_id=device, device_id_type=MESH,
        ).start()

    each(0, 8, send_cells)

    def send_terms():
        owner = place(own_of(me))
        return [
            pltpu.make_async_remote_copy(
                value_ref.at[0], value, send_sem.at[6], value_sem,
                device_id=owner, device_id_type=MESH,
            ),
            pltpu.make_async_remote_copy(
                weight_ref.at[0, 0], weight, send_sem.at[7], weight_sem,
                device_id=owner, device_id_type=MESH,
            ),
        ]

    @pl.when(mine == me)
    def _():
        value[...] = value_ref[0]
        weight[...] = weight_ref[0, 0]

    @pl.when(mine != me)
    def _():
        for copy in send_terms():
            copy.start()

    for step in range(ALONE + 1, FSTEPS + 1):
        inner_step(step)

    def send_field(device, k, b, z):
        pltpu.make_async_remote_copy(
            l8.at[FSTEPS + b], block.at[my_rows, :], send_sem.at[1], field_sem,
            device_id=device, device_id_type=MESH,
        ).start()

    def away_from_edge(z):
        return (z > 0) & (z < 7)

    def send_early(device, k, b, z):
        pl.when(away_from_edge(z))(functools.partial(send_field, device, k, b, z))

    def send_late(device, k, b, z):
        pl.when(jnp.logical_not(away_from_edge(z)))(functools.partial(send_field, device, k, b, z))

    each(1, 1 + EARLY, send_early)

    @pl.when(lat > 0)
    def _():
        for copy in edges(True):
            copy.wait_recv()
        for copy in edges(False):
            copy.wait_send()

    @pl.when(lat < n_lat - 1)
    def _():
        for copy in edges(False):
            copy.wait_recv()
        for copy in edges(True):
            copy.wait_send()

    for step in range(1, FSTEPS + 1):
        for u in range(FSTEPS):
            advance_row(step, step + u)
            advance_row(step, tall - step - FSTEPS + u)

    pltpu.make_async_copy(cells.at[: count - 1], cells.at[: count - 1], cell_sem).wait()

    def observe(i, carry):
        for u in range(8):
            b = i * 8 + u
            index = jnp.broadcast_to(cells[b], lane.shape)
            where, group = jnp.bitwise_and(index, 127), jnp.right_shift(index, 7)
            found = jnp.zeros(lane.shape, F32)
            for p in range(parts):
                picked = jnp.take_along_axis(
                    l8[FSTEPS + b, :, p * 128 : (p + 1) * 128], where, axis=1
                )
                found = jnp.where(group == p, picked, found)
            obs[b] = found
        return carry

    lax.fori_loop(0, count // 8, observe, 0)

    def send_obs(device, k, b, z):
        pltpu.make_async_remote_copy(
            obs.at[b], seen.at[my_rows, :], send_sem.at[0], obs_sem,
            device_id=device, device_id_type=MESH,
        ).start()

    each(0, 8, send_obs)
    each(1, 1 + EARLY, send_late)
    each(1 + EARLY, 1 + AHEAD, send_field)
    seen[my_rows, :] = obs[mine]
    block[my_rows, :] = l8[FSTEPS + mine]

    @pl.when(mine != me)
    def _():
        for copy in send_terms():
            copy.wait()

    others = (count - 1) * per
    pltpu.make_async_copy(seen.at[:others], seen.at[:others], obs_sem).wait()

    ybar = jnp.mean(seen[...], axis=0, keepdims=True)
    own = seen[...] - ybar
    stack[1, :members, :] = own
    stack[1, members:, :] = jnp.broadcast_to(value[...] - ybar, (8, own.shape[1]))

    def to_low():
        return pltpu.make_async_remote_copy(
            stack.at[1], stack.at[2], send_sem.at[2], high_sem,
            device_id=place(own_of(mine - 1)), device_id_type=MESH,
        )

    def to_high():
        return pltpu.make_async_remote_copy(
            stack.at[1], stack.at[0], send_sem.at[3], low_sem,
            device_id=place(own_of(mine + 1)), device_id_type=MESH,
        )

    @pl.when(mine > 0)
    def _():
        to_low().start()

    @pl.when(mine < count - 1)
    def _():
        to_high().start()

    each(1 + AHEAD, 8, send_field)
    each(0, 1, send_field)

    @pl.when(mine == 0)
    def _():
        stack[0] = jnp.zeros(stack.shape[1:], F32)

    @pl.when(mine == count - 1)
    def _():
        stack[2] = jnp.zeros(stack.shape[1:], F32)

    @pl.when(mine > 0)
    def _():
        to_low().wait_send()
        to_high().wait_recv()

    @pl.when(mine < count - 1)
    def _():
        to_high().wait_send()
        to_low().wait_recv()

    obs = own.shape[1]
    pull_row = jnp.zeros((1, members), F32)
    for part in range(3):
        held = stack[part, :members, :]
        weighted = held * weight[pl.ds(part, 1), :]
        pull_row = pull_row + lax.dot_general(
            stack[part, pl.ds(members, 8), :], weighted, (((1,), (1,)), ((), ())),
            precision=lax.Precision.HIGHEST, preferred_element_type=F32,
        )[0:1]
        here = slice(part * obs, (part + 1) * obs)
        wide_hi[:, here], wide_lo[:, here] = split(held)
        left_hi[:, here], left_lo[:, here] = split(weighted)

    rows = 128
    chunks = members // rows

    def eye(start):
        row = lax.broadcasted_iota(jnp.int32, (rows, members), 0) + start
        return (row == lax.broadcasted_iota(jnp.int32, (rows, members), 1)).astype(F32)

    def at(i):
        return pl.ds(pl.multiple_of(i * rows, rows), rows)

    width = 3 * obs

    def gram_rows(i, total):
        part = dot3(
            (left_hi[at(i), :width], left_lo[at(i), :width]),
            (wide_hi[...], wide_lo[...]), ((1,), (1,)),
        )
        part = part / (members - 1) + eye(i * rows)
        gram[at(i), :] = part
        return total + jnp.sum(part * part, keepdims=True)

    total = lax.fori_loop(0, chunks, gram_rows, jnp.zeros((1, 1), F32))
    frobenius = jnp.sqrt(total + 1e-06)

    def scale_rows(i, carry):
        gram[at(i), :] = gram[at(i), :] / frobenius
        return carry

    lax.fori_loop(0, chunks, scale_rows, 0)

    for repeat in range(NS_ITERS):
        last = repeat == NS_ITERS - 1

        def factor_rows(i, carry, repeat=repeat):
            now = gram[at(i), :]
            right_hi[at(i), :], right_lo[at(i), :] = split(1.5 * eye(i * rows) - 0.5 * now)
            left_hi[at(i), :], left_lo[at(i), :] = split(now)
            if repeat == 0:
                inv_hi[at(i), :], inv_lo[at(i), :] = right_hi[at(i), :], right_lo[at(i), :]
            return carry

        lax.fori_loop(0, chunks, factor_rows, 0)

        def step_rows(i, carry, repeat=repeat, last=last):
            right = (right_hi[...], right_lo[...])
            if not last:
                half = dot3((left_hi[at(i), :], left_lo[at(i), :]), right)
                gram[at(i), :] = dot3(split(half), right)
            if repeat > 0:
                inverse = dot3((inv_hi[at(i), :], inv_lo[at(i), :]), right)
                if last:
                    gram[at(i), :] = inverse / jnp.sqrt(frobenius)
                else:
                    inv_hi[at(i), :], inv_lo[at(i), :] = split(inverse)
            return carry

        lax.fori_loop(0, chunks, step_rows, 0)

    inner = jnp.sum(gram[...] * pull_row, axis=1, keepdims=True)
    shift = jnp.sum(gram[...] * inner, axis=0, keepdims=True) / (members - 1)

    spread = 1.0 - jnp.sum(gram[...], axis=1, keepdims=True) - jnp.sum(shift, keepdims=True)
    spread_ref[...] = spread / members

    def cut_rows(i, carry):
        inv_hi[at(i), :], inv_lo[at(i), :] = split(
            gram[at(i), :] + shift + spread_ref[at(i), :]
        )
        return carry

    lax.fori_loop(0, chunks, cut_rows, 0)

    pltpu.make_async_copy(block.at[:others], block.at[:others], field_sem).wait()
    field_hi[...], field_lo[...] = split(block[...])

    group = rows // per
    low_bits = lax.rem(me, group)

    def back(k):
        return pltpu.make_async_remote_copy(
            result.at[pl.ds(pl.multiple_of(k * per, per), per), :], out_ref.at[mine],
            send_sem.at[4], back_sem, device_id=place(k), device_id_type=MESH,
        )

    def final_rows(i, carry):
        c = lax.rem(lax.div(me, group) + i, chunks)
        result[at(c), :] = dot3(
            (inv_hi[at(c), :], inv_lo[at(c), :]), (field_hi[...], field_lo[...])
        )

        for j in range(group):
            k = c * group + lax.rem(low_bits + j, group)

            @pl.when(k != me)
            def _(k=k):
                back(k).start()

        return carry

    lax.fori_loop(0, chunks, final_rows, 0)
    out_ref[mine] = result[my_rows, :]

    pltpu.make_async_copy(out_ref.at[: count - 1], out_ref.at[: count - 1], back_sem).wait()
    pltpu.make_async_copy(seen.at[:others], seen.at[:others], send_sem.at[0]).wait()
    pltpu.make_async_copy(block.at[:others], block.at[:others], send_sem.at[1]).wait()
    pltpu.make_async_copy(block.at[:others], block.at[:others], send_sem.at[4]).wait()
    pltpu.make_async_copy(cells.at[: count - 1], cells.at[: count - 1], send_sem.at[5]).wait()


def whole(state, cx, cy, d, index, value, weight):
    per, count, lon = state.shape
    members, width = count * per, value.shape[2]
    tall = count + 2 * FSTEPS
    square = (members, members)
    return pl.pallas_call(
        whole_kernel,
        out_shape=jax.ShapeDtypeStruct((count, per, lon), F32),
        in_specs=[pl.BlockSpec(memory_space=pl.ANY)] + [VMEM] * 6,
        out_specs=VMEM,
        scratch_shapes=[pltpu.VMEM((tall, per, lon), F32)] * (FSTEPS + 1)
        + [
            pltpu.VMEM((5, count, lon), F32),
            pltpu.VMEM((tall, per, lon), F32),
            pltpu.VMEM((count, 1, width), jnp.int32),
            pltpu.VMEM((count, per, width), F32),
            pltpu.VMEM((1, width), F32),
            pltpu.VMEM((3, width), F32),
            pltpu.VMEM((members, lon), F32),
            pltpu.VMEM((members, width), F32),
            pltpu.VMEM((3, members + 8, width), F32),
            pltpu.VMEM((members, lon), F32),
            pltpu.VMEM((members, 1), F32),
            pltpu.VMEM(square, F32),
        ]
        + [pltpu.VMEM(square, BF16)] * 6
        + [pltpu.VMEM((members, 3 * width), BF16)] * 2
        + [pltpu.VMEM((members, lon), BF16)] * 2
        + [
            pltpu.SemaphoreType.DMA,
            pltpu.SemaphoreType.DMA,
            pltpu.SemaphoreType.DMA((8,)),
            pltpu.SemaphoreType.DMA((2, 2)),
            pltpu.SemaphoreType.DMA((2, 2)),
        ]
        + [pltpu.SemaphoreType.DMA] * 8,
        compiler_params=pltpu.CompilerParams(
            collective_id=0, has_side_effects=True, vmem_limit_bytes=42 << 20
        ),
        cost_estimate=pl.CostEstimate(
            flops=10_000_000_000, bytes_accessed=6_000_000, transcendentals=0
        ),
    )(state, cx, cy, d, index, value, weight)


def on_device(starting_states, courant_x, courant_y, diffusion, obs_index, obs_value, loc_weight):
    out = whole(
        starting_states, courant_x, courant_y, diffusion, obs_index, obs_value, loc_weight
    )
    return jnp.transpose(out, (1, 0, 2))


def solution(mesh):
    in_specs = (
        P(("members", "blk"), "lat", None),
        P("lat", None),
        P("lat", None),
        P("lat", None),
        P("lat", ("members", "blk"), None),
        P("lat", ("members", "blk"), None),
        P("lat", ("members", "blk"), None, None),
    )
    out_specs = P(("members", "blk"), "lat", None)
    return jax.shard_map(
        on_device, mesh=mesh, in_specs=in_specs, out_specs=out_specs, check_vma=False
    )
```

```python
import functools

import jax
import jax.numpy as jnp
from jax import lax
from jax.experimental import pallas as pl
from jax.experimental.pallas import tpu as pltpu
from jax.sharding import PartitionSpec as P

FSTEPS = 8
NS_ITERS = 4
ROWS = 16
EARLY = 0
AHEAD = 2
ALONE = 1
SPIRAL = (1, 7, 2, 6, 3, 5, 4, 0)
MESH = pl.DeviceIdType.MESH
VMEM = pl.BlockSpec(memory_space=pltpu.VMEM)
F32 = jnp.float32
BF16 = jnp.bfloat16


def split(x):
    high = x.astype(BF16)
    return high, (x - high.astype(F32)).astype(BF16)


def dot3(a, b, contract=((1,), (0,))):
    def one(p, q):
        return lax.dot_general(p, q, (contract, ((), ())), preferred_element_type=F32)

    return one(a[0], b[0]) + (one(a[0], b[1]) + one(a[1], b[0]))


def whole_kernel(
    state_ref, cx_ref, cy_ref, d_ref, index_ref, value_ref, weight_ref, out_ref,
    l0, l1, l2, l3, l4, l5, l6, l7, l8,
    raw, dense, coef, cells, obs, value, weight, block, seen, stack, result,
    spread_ref, gram, left_hi, left_lo, right_hi, right_lo, inv_hi, inv_lo, wide_hi, wide_lo, field_hi, field_lo,
    load_sem, raw_sem, coef_sem, own_sem, send_sem, edge_send, edge_recv,
    cell_sem, value_sem, weight_sem, obs_sem, field_sem, low_sem, high_sem, back_sem,
):
    levels = (l0, l1, l2, l3, l4, l5, l6, l7, l8)
    per, count, lon = state_ref.shape
    members = count * per
    tall = count + 2 * FSTEPS
    lo = lax.axis_index("members")
    bl = lax.axis_index("blk")
    lat = lax.axis_index("lat")
    n_lat = lax.axis_size("lat")
    n_blk = lax.axis_size("blk")
    me = lo * n_blk + bl
    my_z, my_y, my_core = (lo // 8) * 4 + bl, (lo // 2) % 4, lo % 2

    def set_at(z, y, core):
        return (((z // 4) * 4 + y) * 2 + core) * 4 + z % 4

    def block_at(z, y, core):
        return (z * 4 + y + (z % 2) * (3 - 2 * y)) * 2 + core

    def own_of(b):
        z, y = b // 8, (b // 2) % 4
        return set_at(z, y + (z % 2) * (3 - 2 * y), b % 2)

    def place(k):
        return {"members": k // n_blk, "blk": k % n_blk}

    zs = [lax.rem(my_z + dz, 8) for dz in range(8)]
    z_sets = [lax.div(z, 4) * 8 for z in zs]
    z_blks = [lax.rem(z, 4) for z in zs]

    def each(first, last, act):
        def group(q, carry):
            y = lax.rem(my_y + lax.div(q, 2), 4)
            core = lax.rem(my_core + lax.rem(q, 2), 2)
            even, odd = y * 2 + core, (3 - y) * 2 + core
            for dz in SPIRAL:
                z = zs[dz]
                m, blk = z_sets[dz] + even, z_blks[dz]
                b = z * 8 + even + lax.rem(z, 2) * (odd - even)
                run = functools.partial(act, {"members": m, "blk": blk}, m * 4 + blk, b, z)
                if dz == 0:
                    pl.when(q > 0)(run)
                else:
                    run()
            return carry

        lax.fori_loop(first, last, group, 0)

    mine = block_at(my_z, my_y, my_core)
    my_rows = pl.ds(pl.multiple_of(me * per, per), per)
    inner = pl.ds(FSTEPS, count)

    for i, ref in enumerate((cx_ref, cy_ref, d_ref)):
        pltpu.make_async_copy(ref, raw.at[i], raw_sem).start()
    pltpu.make_async_copy(index_ref.at[0], cells.at[me], own_sem.at[0]).start()
    for m in range(per):
        pltpu.make_async_copy(state_ref.at[m], l0.at[inner, m, :], load_sem).start()

    barrier = pltpu.get_barrier_semaphore()

    @pl.when(lat > 0)
    def _():
        pl.semaphore_signal(barrier, inc=1, device_id={"lat": lat - 1}, device_id_type=MESH)

    @pl.when(lat < n_lat - 1)
    def _():
        pl.semaphore_signal(barrier, inc=1, device_id={"lat": lat + 1}, device_id_type=MESH)

    def greet(device, k, b, z):
        pl.semaphore_signal(barrier, inc=1, device_id=device, device_id_type=MESH)

    each(0, 8, greet)

    pltpu.make_async_copy(raw, raw, raw_sem).wait()
    cx, cy, d = 0.5 * raw[0], 0.5 * raw[1], raw[2]
    for i, term in enumerate((1.0 - 4.0 * d, d - cx, d + cx, d - cy, d + cy)):
        dense[i] = term
        pltpu.make_async_copy(dense.at[i], coef.at[inner, i, :], coef_sem).start()
    low_rows, high_rows = pl.ds(0, FSTEPS), pl.ds(FSTEPS + count, FSTEPS)

    @pl.when(lat == 0)
    def _():
        l0[low_rows] = jnp.zeros((FSTEPS, per, lon), F32)
        coef[low_rows] = jnp.zeros((FSTEPS, per, lon), F32)

    @pl.when(lat == n_lat - 1)
    def _():
        l0[high_rows] = jnp.zeros((FSTEPS, per, lon), F32)
        coef[high_rows] = jnp.zeros((FSTEPS, per, lon), F32)

    lane = lax.broadcasted_iota(jnp.int32, (per, 128), 1)
    parts = lon // 128

    def advance_row(step, r):
        old, new = levels[step - 1], levels[step]
        pieces = [old[r, :, p * 128 : (p + 1) * 128] for p in range(parts)]
        right = [pltpu.roll(v, 1, 1) for v in pieces]
        left = [pltpu.roll(v, 127, 1) for v in pieces]
        for p in range(parts):
            here = slice(p * 128, (p + 1) * 128)
            west = jnp.where(lane == 0, right[p - 1], right[p])
            east = jnp.where(lane == 127, left[(p + 1) % parts], left[p])
            c = [jnp.broadcast_to(coef[r, pl.ds(i, 1), here], lane.shape) for i in range(5)]
            new[r, :, here] = (
                (c[0] * pieces[p] + c[1] * east)
                + (c[2] * west + c[3] * old[r + 1, :, here])
                + c[4] * old[r - 1, :, here]
            )

    def inner_step(step):
        low, high = FSTEPS + step, FSTEPS + count - step

        def rows(i, carry):
            start = jnp.minimum(low + ROWS * i, high - ROWS)
            for u in range(ROWS):
                advance_row(step, start + u)
            return carry

        lax.fori_loop(0, (high - low + ROWS - 1) // ROWS, rows, 0)

    pltpu.make_async_copy(l0.at[inner], l0.at[inner], load_sem).wait()
    pltpu.make_async_copy(dense, dense, coef_sem).wait()
    for step in range(1, ALONE + 1):
        inner_step(step)
    pl.semaphore_wait(
        barrier, count - 1 + jnp.where(lat > 0, 1, 0) + jnp.where(lat < n_lat - 1, 1, 0)
    )

    def edges(up):
        source = pl.ds(count if up else FSTEPS, FSTEPS)
        target = low_rows if up else high_rows
        side = 0 if up else 1
        device = {"lat": lat + 1 if up else lat - 1}
        return [
            pltpu.make_async_remote_copy(
                l0.at[source], l0.at[target], edge_send.at[side, 0], edge_recv.at[side, 0],
                device_id=device, device_id_type=MESH,
            ),
            pltpu.make_async_remote_copy(
                coef.at[source, 0:5, :], coef.at[target, 0:5, :], edge_send.at[side, 1],
                edge_recv.at[side, 1], device_id=device, device_id_type=MESH,
            ),
        ]

    @pl.when(lat < n_lat - 1)
    def _():
        for copy in edges(True):
            copy.start()

    @pl.when(lat > 0)
    def _():
        for copy in edges(False):
            copy.start()

    def send_cells(device, k, b, z):
        pltpu.make_async_remote_copy(
            index_ref.at[0], cells.at[me], send_sem.at[5], cell_sem,
            device_id=device, device_id_type=MESH,
        ).start()

    each(0, 8, send_cells)

    def send_terms():
        owner = place(own_of(me))
        return [
            pltpu.make_async_remote_copy(
                value_ref.at[0], value, send_sem.at[6], value_sem,
                device_id=owner, device_id_type=MESH,
            ),
            pltpu.make_async_remote_copy(
                weight_ref, weight, send_sem.at[7], weight_sem,
                device_id=owner, device_id_type=MESH,
            ),
        ]

    def keep_terms():
        return [
            pltpu.make_async_copy(value_ref.at[0], value, own_sem.at[1]),
            pltpu.make_async_copy(weight_ref, weight, own_sem.at[2]),
        ]

    @pl.when(mine == me)
    def _():
        for copy in keep_terms():
            copy.start()

    @pl.when(mine != me)
    def _():
        for copy in send_terms():
            copy.start()

    for step in range(ALONE + 1, FSTEPS + 1):
        inner_step(step)

    def send_field(device, k, b, z):
        pltpu.make_async_remote_copy(
            l8.at[FSTEPS + b], block.at[my_rows, :], send_sem.at[1], field_sem,
            device_id=device, device_id_type=MESH,
        ).start()

    def away_from_edge(z):
        return (z > 0) & (z < 7)

    def send_early(device, k, b, z):
        pl.when(away_from_edge(z))(functools.partial(send_field, device, k, b, z))

    def send_late(device, k, b, z):
        pl.when(jnp.logical_not(away_from_edge(z)))(functools.partial(send_field, device, k, b, z))

    each(1, 1 + EARLY, send_early)

    @pl.when(lat > 0)
    def _():
        for copy in edges(True):
            copy.wait_recv()
        for copy in edges(False):
            copy.wait_send()

    @pl.when(lat < n_lat - 1)
    def _():
        for copy in edges(False):
            copy.wait_recv()
        for copy in edges(True):
            copy.wait_send()

    for step in range(1, FSTEPS + 1):
        for u in range(FSTEPS):
            advance_row(step, step + u)
            advance_row(step, tall - step - FSTEPS + u)

    pltpu.make_async_copy(cells.at[: count - 1], cells.at[: count - 1], cell_sem).wait()
    pltpu.make_async_copy(index_ref.at[0], cells.at[me], own_sem.at[0]).wait()

    def observe(i, carry):
        for u in range(8):
            b = i * 8 + u
            index = jnp.broadcast_to(cells[b], lane.shape)
            where, group = jnp.bitwise_and(index, 127), jnp.right_shift(index, 7)
            found = jnp.zeros(lane.shape, F32)
            for p in range(parts):
                picked = jnp.take_along_axis(
                    l8[FSTEPS + b, :, p * 128 : (p + 1) * 128], where, axis=1
                )
                found = jnp.where(group == p, picked, found)
            obs[b] = found
        return carry

    lax.fori_loop(0, count // 8, observe, 0)

    def send_obs(device, k, b, z):
        pltpu.make_async_remote_copy(
            obs.at[b], seen.at[my_rows, :], send_sem.at[0], obs_sem,
            device_id=device, device_id_type=MESH,
        ).start()

    each(0, 8, send_obs)
    each(1, 1 + EARLY, send_late)
    each(1 + EARLY, 1 + AHEAD, send_field)
    seen[my_rows, :] = obs[mine]
    block[my_rows, :] = l8[FSTEPS + mine]

    @pl.when(mine != me)
    def _():
        for copy in send_terms():
            copy.wait()

    @pl.when(mine == me)
    def _():
        for copy in keep_terms():
            copy.wait()

    others = (count - 1) * per
    pltpu.make_async_copy(seen.at[:others], seen.at[:others], obs_sem).wait()

    ybar = jnp.mean(seen[...], axis=0, keepdims=True)
    own = seen[...] - ybar
    stack[1, :members, :] = own
    stack[1, members:, :] = jnp.broadcast_to(value[...] - ybar, (8, own.shape[1]))

    def to_low():
        return pltpu.make_async_remote_copy(
            stack.at[1], stack.at[2], send_sem.at[2], high_sem,
            device_id=place(own_of(mine - 1)), device_id_type=MESH,
        )

    def to_high():
        return pltpu.make_async_remote_copy(
            stack.at[1], stack.at[0], send_sem.at[3], low_sem,
            device_id=place(own_of(mine + 1)), device_id_type=MESH,
        )

    @pl.when(mine > 0)
    def _():
        to_low().start()

    @pl.when(mine < count - 1)
    def _():
        to_high().start()

    each(1 + AHEAD, 8, send_field)
    each(0, 1, send_field)

    @pl.when(mine == 0)
    def _():
        stack[0] = jnp.zeros(stack.shape[1:], F32)

    @pl.when(mine == count - 1)
    def _():
        stack[2] = jnp.zeros(stack.shape[1:], F32)

    @pl.when(mine > 0)
    def _():
        to_low().wait_send()
        to_high().wait_recv()

    @pl.when(mine < count - 1)
    def _():
        to_high().wait_send()
        to_low().wait_recv()

    obs = own.shape[1]
    pull_row = jnp.zeros((1, members), F32)
    for part in range(3):
        held = stack[part, :members, :]
        weighted = held * weight[part]
        pull_row = pull_row + lax.dot_general(
            stack[part, pl.ds(members, 8), :], weighted, (((1,), (1,)), ((), ())),
            precision=lax.Precision.HIGHEST, preferred_element_type=F32,
        )[0:1]
        here = slice(part * obs, (part + 1) * obs)
        wide_hi[:, here], wide_lo[:, here] = split(held)
        left_hi[:, here], left_lo[:, here] = split(weighted)

    rows = 256
    chunks = members // rows

    def eye(start):
        row = lax.broadcasted_iota(jnp.int32, (rows, members), 0) + start
        return (row == lax.broadcasted_iota(jnp.int32, (rows, members), 1)).astype(F32)

    def at(i):
        return pl.ds(pl.multiple_of(i * rows, rows), rows)

    width = 3 * obs

    def gram_rows(i, total):
        part = dot3(
            (left_hi[at(i), :width], left_lo[at(i), :width]),
            (wide_hi[...], wide_lo[...]), ((1,), (1,)),
        )
        part = part / (members - 1) + eye(i * rows)
        gram[at(i), :] = part
        return total + jnp.sum(part * part, keepdims=True)

    total = lax.fori_loop(0, chunks, gram_rows, jnp.zeros((1, 1), F32))
    frobenius = jnp.sqrt(total + 1e-06)

    def scale_rows(i, carry):
        gram[at(i), :] = gram[at(i), :] / frobenius
        return carry

    lax.fori_loop(0, chunks, scale_rows, 0)

    for repeat in range(NS_ITERS):
        last = repeat == NS_ITERS - 1

        def factor_rows(i, carry, repeat=repeat):
            now = gram[at(i), :]
            right_hi[at(i), :], right_lo[at(i), :] = split(1.5 * eye(i * rows) - 0.5 * now)
            left_hi[at(i), :], left_lo[at(i), :] = split(now)
            if repeat == 0:
                inv_hi[at(i), :], inv_lo[at(i), :] = right_hi[at(i), :], right_lo[at(i), :]
            return carry

        lax.fori_loop(0, chunks, factor_rows, 0)

        def step_rows(i, carry, repeat=repeat, last=last):
            right = (right_hi[...], right_lo[...])
            if not last:
                half = dot3((left_hi[at(i), :], left_lo[at(i), :]), right)
                gram[at(i), :] = dot3(split(half), right)
            if repeat > 0:
                inverse = dot3((inv_hi[at(i), :], inv_lo[at(i), :]), right)
                if last:
                    gram[at(i), :] = inverse / jnp.sqrt(frobenius)
                else:
                    inv_hi[at(i), :], inv_lo[at(i), :] = split(inverse)
            return carry

        lax.fori_loop(0, chunks, step_rows, 0)

    inner = jnp.sum(gram[...] * pull_row, axis=1, keepdims=True)
    shift = jnp.sum(gram[...] * inner, axis=0, keepdims=True) / (members - 1)

    spread = 1.0 - jnp.sum(gram[...], axis=1, keepdims=True) - jnp.sum(shift, keepdims=True)
    spread_ref[...] = spread / members

    def cut_rows(i, carry):
        inv_hi[at(i), :], inv_lo[at(i), :] = split(
            gram[at(i), :] + shift + spread_ref[at(i), :]
        )
        return carry

    lax.fori_loop(0, chunks, cut_rows, 0)

    pltpu.make_async_copy(block.at[:others], block.at[:others], field_sem).wait()
    field_hi[...], field_lo[...] = split(block[...])

    rows = 128
    chunks = members // rows
    group = rows // per
    low_bits = lax.rem(me, group)

    def back(k):
        return pltpu.make_async_remote_copy(
            result.at[pl.ds(pl.multiple_of(k * per, per), per), :], out_ref.at[mine],
            send_sem.at[4], back_sem, device_id=place(k), device_id_type=MESH,
        )

    def final_rows(i, carry):
        c = lax.rem(lax.div(me, group) + i, chunks)
        result[at(c), :] = dot3(
            (inv_hi[at(c), :], inv_lo[at(c), :]), (field_hi[...], field_lo[...])
        )

        for j in range(group):
            k = c * group + lax.rem(low_bits + j, group)

            @pl.when(k != me)
            def _(k=k):
                back(k).start()

        return carry

    lax.fori_loop(0, chunks, final_rows, 0)
    out_ref[mine] = result[my_rows, :]

    pltpu.make_async_copy(out_ref.at[: count - 1], out_ref.at[: count - 1], back_sem).wait()
    pltpu.make_async_copy(seen.at[:others], seen.at[:others], send_sem.at[0]).wait()
    pltpu.make_async_copy(block.at[:others], block.at[:others], send_sem.at[1]).wait()
    pltpu.make_async_copy(block.at[:others], block.at[:others], send_sem.at[4]).wait()
    pltpu.make_async_copy(cells.at[: count - 1], cells.at[: count - 1], send_sem.at[5]).wait()


def whole(state, cx, cy, d, index, value, weight):
    per, count, lon = state.shape
    members, width = count * per, value.shape[2]
    tall = count + 2 * FSTEPS
    square = (members, members)
    state, cx, cy, d, index, value, weight = [
        pltpu.with_memory_space_constraint(x, pltpu.HBM)
        for x in (state, cx, cy, d, index, value, weight)
    ]
    return pl.pallas_call(
        whole_kernel,
        out_shape=jax.ShapeDtypeStruct((count, per, lon), F32),
        in_specs=[pl.BlockSpec(memory_space=pltpu.HBM)] * 7,
        out_specs=VMEM,
        scratch_shapes=[pltpu.VMEM((tall, per, lon), F32)] * (FSTEPS + 1)
        + [
            pltpu.VMEM((3, count, lon), F32),
            pltpu.VMEM((5, count, lon), F32),
            pltpu.VMEM((tall, per, lon), F32),
            pltpu.VMEM((count, 1, width), jnp.int32),
            pltpu.VMEM((count, per, width), F32),
            pltpu.VMEM((1, width), F32),
            pltpu.VMEM((3, 1, width), F32),
            pltpu.VMEM((members, lon), F32),
            pltpu.VMEM((members, width), F32),
            pltpu.VMEM((3, members + 8, width), F32),
            pltpu.VMEM((members, lon), F32),
            pltpu.VMEM((members, 1), F32),
            pltpu.VMEM(square, F32),
        ]
        + [pltpu.VMEM(square, BF16)] * 6
        + [pltpu.VMEM((members, 3 * width), BF16)] * 2
        + [pltpu.VMEM((members, lon), BF16)] * 2
        + [
            pltpu.SemaphoreType.DMA,
            pltpu.SemaphoreType.DMA,
            pltpu.SemaphoreType.DMA,
            pltpu.SemaphoreType.DMA((3,)),
            pltpu.SemaphoreType.DMA((8,)),
            pltpu.SemaphoreType.DMA((2, 2)),
            pltpu.SemaphoreType.DMA((2, 2)),
        ]
        + [pltpu.SemaphoreType.DMA] * 8,
        compiler_params=pltpu.CompilerParams(
            collective_id=0, has_side_effects=True, vmem_limit_bytes=42 << 20
        ),
        cost_estimate=pl.CostEstimate(
            flops=10_000_000_000, bytes_accessed=6_000_000, transcendentals=0
        ),
    )(state, cx, cy, d, index, value, weight)


def on_device(starting_states, courant_x, courant_y, diffusion, obs_index, obs_value, loc_weight):
    out = whole(
        starting_states, courant_x, courant_y, diffusion, obs_index, obs_value,
        loc_weight.reshape(3, 1, -1),
    )
    return jnp.transpose(out, (1, 0, 2))


def solution(mesh):
    in_specs = (
        P(("members", "blk"), "lat", None),
        P("lat", None),
        P("lat", None),
        P("lat", None),
        P("lat", ("members", "blk"), None),
        P("lat", ("members", "blk"), None),
        P("lat", ("members", "blk"), None, None),
    )
    out_specs = P(("members", "blk"), "lat", None)
    return jax.shard_map(
        on_device, mesh=mesh, in_specs=in_specs, out_specs=out_specs, check_vma=False
    )
```

```python
import functools

import jax
import jax.numpy as jnp
from jax import lax
from jax.experimental import pallas as pl
from jax.experimental.pallas import tpu as pltpu
from jax.sharding import PartitionSpec as P

FSTEPS = 8
NS_ITERS = 4
ROWS = 16
EARLY = 2
AHEAD = 2
ALONE = 1
SPIRAL = (1, 7, 2, 6, 3, 5, 4, 0)
MESH = pl.DeviceIdType.MESH
VMEM = pl.BlockSpec(memory_space=pltpu.VMEM)
F32 = jnp.float32
BF16 = jnp.bfloat16


def split(x):
    high = x.astype(BF16)
    return high, (x - high.astype(F32)).astype(BF16)


def dot3(a, b, contract=((1,), (0,))):
    def one(p, q):
        return lax.dot_general(p, q, (contract, ((), ())), preferred_element_type=F32)

    return one(a[0], b[0]) + (one(a[0], b[1]) + one(a[1], b[0]))


def whole_kernel(
    state_ref, cx_ref, cy_ref, d_ref, index_ref, value_ref, weight_ref, out_ref,
    l0, l1, l2, l3, l4, l5, l6, l7, l8,
    raw, dense, coef, cells, obs, value, weight, block, seen, stack, result,
    spread_ref, gram, left_hi, left_lo, right_hi, right_lo, inv_hi, inv_lo, wide_hi, wide_lo, field_hi, field_lo,
    load_sem, raw_sem, coef_sem, own_sem, send_sem, edge_send, edge_recv,
    cell_sem, value_sem, weight_sem, obs_sem, field_sem, low_sem, high_sem, back_sem,
):
    levels = (l0, l1, l2, l3, l4, l5, l6, l7, l8)
    per, count, lon = state_ref.shape
    members = count * per
    tall = count + 2 * FSTEPS
    lo = lax.axis_index("members")
    bl = lax.axis_index("blk")
    lat = lax.axis_index("lat")
    n_lat = lax.axis_size("lat")
    n_blk = lax.axis_size("blk")
    me = lo * n_blk + bl
    my_z, my_y, my_core = (lo // 8) * 4 + bl, (lo // 2) % 4, lo % 2

    def set_at(z, y, core):
        return (((z // 4) * 4 + y) * 2 + core) * 4 + z % 4

    def block_at(z, y, core):
        return (z * 4 + y + (z % 2) * (3 - 2 * y)) * 2 + core

    def own_of(b):
        z, y = b // 8, (b // 2) % 4
        return set_at(z, y + (z % 2) * (3 - 2 * y), b % 2)

    def place(k):
        return {"members": k // n_blk, "blk": k % n_blk}

    zs = [lax.rem(my_z + dz, 8) for dz in range(8)]
    z_sets = [lax.div(z, 4) * 8 for z in zs]
    z_blks = [lax.rem(z, 4) for z in zs]

    def each(first, last, act):
        def group(q, carry):
            y = lax.rem(my_y + lax.div(q, 2), 4)
            core = lax.rem(my_core + lax.rem(q, 2), 2)
            even, odd = y * 2 + core, (3 - y) * 2 + core
            for dz in SPIRAL:
                z = zs[dz]
                m, blk = z_sets[dz] + even, z_blks[dz]
                b = z * 8 + even + lax.rem(z, 2) * (odd - even)
                run = functools.partial(act, {"members": m, "blk": blk}, m * 4 + blk, b, z)
                if dz == 0:
                    pl.when(q > 0)(run)
                else:
                    run()
            return carry

        lax.fori_loop(first, last, group, 0)

    mine = block_at(my_z, my_y, my_core)
    my_rows = pl.ds(pl.multiple_of(me * per, per), per)
    inner = pl.ds(FSTEPS, count)

    for i, ref in enumerate((cx_ref, cy_ref, d_ref)):
        pltpu.make_async_copy(ref, raw.at[i], raw_sem).start()
    pltpu.make_async_copy(index_ref.at[0], cells.at[me], own_sem.at[0]).start()
    for m in range(per):
        pltpu.make_async_copy(state_ref.at[m], l0.at[inner, m, :], load_sem).start()

    barrier = pltpu.get_barrier_semaphore()

    @pl.when(lat > 0)
    def _():
        pl.semaphore_signal(barrier, inc=1, device_id={"lat": lat - 1}, device_id_type=MESH)

    @pl.when(lat < n_lat - 1)
    def _():
        pl.semaphore_signal(barrier, inc=1, device_id={"lat": lat + 1}, device_id_type=MESH)

    def greet(device, k, b, z):
        pl.semaphore_signal(barrier, inc=1, device_id=device, device_id_type=MESH)

    each(0, 8, greet)

    pltpu.make_async_copy(raw, raw, raw_sem).wait()
    cx, cy, d = 0.5 * raw[0], 0.5 * raw[1], raw[2]
    for i, term in enumerate((1.0 - 4.0 * d, d - cx, d + cx, d - cy, d + cy)):
        dense[i] = term
        pltpu.make_async_copy(dense.at[i], coef.at[inner, i, :], coef_sem).start()
    low_rows, high_rows = pl.ds(0, FSTEPS), pl.ds(FSTEPS + count, FSTEPS)

    @pl.when(lat == 0)
    def _():
        l0[low_rows] = jnp.zeros((FSTEPS, per, lon), F32)
        coef[low_rows] = jnp.zeros((FSTEPS, per, lon), F32)

    @pl.when(lat == n_lat - 1)
    def _():
        l0[high_rows] = jnp.zeros((FSTEPS, per, lon), F32)
        coef[high_rows] = jnp.zeros((FSTEPS, per, lon), F32)

    lane = lax.broadcasted_iota(jnp.int32, (per, 128), 1)
    parts = lon // 128

    def advance_row(step, r):
        old, new = levels[step - 1], levels[step]
        pieces = [old[r, :, p * 128 : (p + 1) * 128] for p in range(parts)]
        right = [pltpu.roll(v, 1, 1) for v in pieces]
        left = [pltpu.roll(v, 127, 1) for v in pieces]
        for p in range(parts):
            here = slice(p * 128, (p + 1) * 128)
            west = jnp.where(lane == 0, right[p - 1], right[p])
            east = jnp.where(lane == 127, left[(p + 1) % parts], left[p])
            c = [jnp.broadcast_to(coef[r, pl.ds(i, 1), here], lane.shape) for i in range(5)]
            new[r, :, here] = (
                (c[0] * pieces[p] + c[1] * east)
                + (c[2] * west + c[3] * old[r + 1, :, here])
                + c[4] * old[r - 1, :, here]
            )

    def inner_step(step):
        low, high = FSTEPS + step, FSTEPS + count - step

        def rows(i, carry):
            start = jnp.minimum(low + ROWS * i, high - ROWS)
            for u in range(ROWS):
                advance_row(step, start + u)
            return carry

        lax.fori_loop(0, (high - low + ROWS - 1) // ROWS, rows, 0)

    pltpu.make_async_copy(l0.at[inner], l0.at[inner], load_sem).wait()
    pltpu.make_async_copy(dense, dense, coef_sem).wait()
    for step in range(1, ALONE + 1):
        inner_step(step)
    pl.semaphore_wait(
        barrier, count - 1 + jnp.where(lat > 0, 1, 0) + jnp.where(lat < n_lat - 1, 1, 0)
    )

    def edges(up):
        source = pl.ds(count if up else FSTEPS, FSTEPS)
        target = low_rows if up else high_rows
        side = 0 if up else 1
        device = {"lat": lat + 1 if up else lat - 1}
        return [
            pltpu.make_async_remote_copy(
                l0.at[source], l0.at[target], edge_send.at[side, 0], edge_recv.at[side, 0],
                device_id=device, device_id_type=MESH,
            ),
            pltpu.make_async_remote_copy(
                coef.at[source, 0:5, :], coef.at[target, 0:5, :], edge_send.at[side, 1],
                edge_recv.at[side, 1], device_id=device, device_id_type=MESH,
            ),
        ]

    def send_cells(device, k, b, z):
        pltpu.make_async_remote_copy(
            index_ref.at[0], cells.at[me], send_sem.at[5], cell_sem,
            device_id=device, device_id_type=MESH,
        ).start()

    each(0, 8, send_cells)

    @pl.when(lat < n_lat - 1)
    def _():
        for copy in edges(True):
            copy.start()

    @pl.when(lat > 0)
    def _():
        for copy in edges(False):
            copy.start()


    def send_terms():
        owner = place(own_of(me))
        return [
            pltpu.make_async_remote_copy(
                value_ref.at[0], value, send_sem.at[6], value_sem,
                device_id=owner, device_id_type=MESH,
            ),
            pltpu.make_async_remote_copy(
                weight_ref, weight, send_sem.at[7], weight_sem,
                device_id=owner, device_id_type=MESH,
            ),
        ]

    def keep_terms():
        return [
            pltpu.make_async_copy(value_ref.at[0], value, own_sem.at[1]),
            pltpu.make_async_copy(weight_ref, weight, own_sem.at[2]),
        ]

    @pl.when(mine == me)
    def _():
        for copy in keep_terms():
            copy.start()

    @pl.when(mine != me)
    def _():
        for copy in send_terms():
            copy.start()

    for step in range(ALONE + 1, FSTEPS + 1):
        inner_step(step)

    def send_field(device, k, b, z):
        pltpu.make_async_remote_copy(
            l8.at[FSTEPS + b], block.at[my_rows, :], send_sem.at[1], field_sem,
            device_id=device, device_id_type=MESH,
        ).start()

    def away_from_edge(z):
        return (z > 0) & (z < 7)

    def send_early(device, k, b, z):
        pl.when(away_from_edge(z))(functools.partial(send_field, device, k, b, z))

    def send_late(device, k, b, z):
        pl.when(jnp.logical_not(away_from_edge(z)))(functools.partial(send_field, device, k, b, z))

    pltpu.make_async_copy(cells.at[: count - 1], cells.at[: count - 1], cell_sem).wait()
    pltpu.make_async_copy(index_ref.at[0], cells.at[me], own_sem.at[0]).wait()

    def observe(i, carry):
        for u in range(8):
            b = i * 8 + u
            index = jnp.broadcast_to(cells[b], lane.shape)
            where, group = jnp.bitwise_and(index, 127), jnp.right_shift(index, 7)
            found = jnp.zeros(lane.shape, F32)
            for p in range(parts):
                picked = jnp.take_along_axis(
                    l8[FSTEPS + b, :, p * 128 : (p + 1) * 128], where, axis=1
                )
                found = jnp.where(group == p, picked, found)
            obs[b] = found
        return carry

    lax.fori_loop(1, count // 8 - 1, observe, 0)

    def send_obs(device, k, b, z):
        pltpu.make_async_remote_copy(
            obs.at[b], seen.at[my_rows, :], send_sem.at[0], obs_sem,
            device_id=device, device_id_type=MESH,
        ).start()

    def send_inner_obs(device, k, b, z):
        pl.when(away_from_edge(z))(functools.partial(send_obs, device, k, b, z))

    def send_edge_obs(device, k, b, z):
        pl.when(jnp.logical_not(away_from_edge(z)))(functools.partial(send_obs, device, k, b, z))

    each(0, 8, send_inner_obs)
    each(1, 1 + EARLY, send_early)

    @pl.when(lat > 0)
    def _():
        for copy in edges(True):
            copy.wait_recv()
        for copy in edges(False):
            copy.wait_send()

    @pl.when(lat < n_lat - 1)
    def _():
        for copy in edges(False):
            copy.wait_recv()
        for copy in edges(True):
            copy.wait_send()

    for step in range(1, FSTEPS + 1):
        for u in range(FSTEPS):
            advance_row(step, step + u)
            advance_row(step, tall - step - FSTEPS + u)

    lax.fori_loop(0, 1, observe, 0)
    lax.fori_loop(count // 8 - 1, count // 8, observe, 0)

    each(0, 8, send_edge_obs)
    each(1, 1 + EARLY, send_late)
    each(1 + EARLY, 1 + AHEAD, send_field)
    seen[my_rows, :] = obs[mine]
    block[my_rows, :] = l8[FSTEPS + mine]

    @pl.when(mine != me)
    def _():
        for copy in send_terms():
            copy.wait()

    @pl.when(mine == me)
    def _():
        for copy in keep_terms():
            copy.wait()

    others = (count - 1) * per
    pltpu.make_async_copy(seen.at[:others], seen.at[:others], obs_sem).wait()

    ybar = jnp.mean(seen[...], axis=0, keepdims=True)
    own = seen[...] - ybar
    stack[1, :members, :] = own
    stack[1, members:, :] = jnp.broadcast_to(value[...] - ybar, (8, own.shape[1]))

    def to_low():
        return pltpu.make_async_remote_copy(
            stack.at[1], stack.at[2], send_sem.at[2], high_sem,
            device_id=place(own_of(mine - 1)), device_id_type=MESH,
        )

    def to_high():
        return pltpu.make_async_remote_copy(
            stack.at[1], stack.at[0], send_sem.at[3], low_sem,
            device_id=place(own_of(mine + 1)), device_id_type=MESH,
        )

    @pl.when(mine > 0)
    def _():
        to_low().start()

    @pl.when(mine < count - 1)
    def _():
        to_high().start()

    each(1 + AHEAD, 8, send_field)
    each(0, 1, send_field)

    @pl.when(mine == 0)
    def _():
        stack[0] = jnp.zeros(stack.shape[1:], F32)

    @pl.when(mine == count - 1)
    def _():
        stack[2] = jnp.zeros(stack.shape[1:], F32)

    @pl.when(mine > 0)
    def _():
        to_low().wait_send()
        to_high().wait_recv()

    @pl.when(mine < count - 1)
    def _():
        to_high().wait_send()
        to_low().wait_recv()

    obs = own.shape[1]
    pull_row = jnp.zeros((1, members), F32)
    for part in range(3):
        held = stack[part, :members, :]
        weighted = held * weight[part]
        pull_row = pull_row + lax.dot_general(
            stack[part, pl.ds(members, 8), :], weighted, (((1,), (1,)), ((), ())),
            precision=lax.Precision.HIGHEST, preferred_element_type=F32,
        )[0:1]
        here = slice(part * obs, (part + 1) * obs)
        wide_hi[:, here], wide_lo[:, here] = split(held)
        left_hi[:, here], left_lo[:, here] = split(weighted)

    rows = 256
    chunks = members // rows

    def eye(start):
        row = lax.broadcasted_iota(jnp.int32, (rows, members), 0) + start
        return (row == lax.broadcasted_iota(jnp.int32, (rows, members), 1)).astype(F32)

    def at(i):
        return pl.ds(pl.multiple_of(i * rows, rows), rows)

    width = 3 * obs

    def gram_rows(i, total):
        part = dot3(
            (left_hi[at(i), :width], left_lo[at(i), :width]),
            (wide_hi[...], wide_lo[...]), ((1,), (1,)),
        )
        part = part / (members - 1) + eye(i * rows)
        gram[at(i), :] = part
        return total + jnp.sum(part * part, keepdims=True)

    total = lax.fori_loop(0, chunks, gram_rows, jnp.zeros((1, 1), F32))
    frobenius = jnp.sqrt(total + 1e-06)

    def scale_rows(i, carry):
        gram[at(i), :] = gram[at(i), :] / frobenius
        return carry

    lax.fori_loop(0, chunks, scale_rows, 0)

    for repeat in range(NS_ITERS):
        last = repeat == NS_ITERS - 1

        def factor_rows(i, carry, repeat=repeat):
            now = gram[at(i), :]
            right_hi[at(i), :], right_lo[at(i), :] = split(1.5 * eye(i * rows) - 0.5 * now)
            left_hi[at(i), :], left_lo[at(i), :] = split(now)
            if repeat == 0:
                inv_hi[at(i), :], inv_lo[at(i), :] = right_hi[at(i), :], right_lo[at(i), :]
            return carry

        lax.fori_loop(0, chunks, factor_rows, 0)

        def step_rows(i, carry, repeat=repeat, last=last):
            right = (right_hi[...], right_lo[...])
            if not last:
                half = dot3((left_hi[at(i), :], left_lo[at(i), :]), right)
                gram[at(i), :] = dot3(split(half), right)
            if repeat > 0:
                inverse = dot3((inv_hi[at(i), :], inv_lo[at(i), :]), right)
                if last:
                    gram[at(i), :] = inverse / jnp.sqrt(frobenius)
                else:
                    inv_hi[at(i), :], inv_lo[at(i), :] = split(inverse)
            return carry

        lax.fori_loop(0, chunks, step_rows, 0)

    inner = jnp.sum(gram[...] * pull_row, axis=1, keepdims=True)
    shift = jnp.sum(gram[...] * inner, axis=0, keepdims=True) / (members - 1)

    spread = 1.0 - jnp.sum(gram[...], axis=1, keepdims=True) - jnp.sum(shift, keepdims=True)
    spread_ref[...] = spread / members

    def cut_rows(i, carry):
        inv_hi[at(i), :], inv_lo[at(i), :] = split(
            gram[at(i), :] + shift + spread_ref[at(i), :]
        )
        return carry

    lax.fori_loop(0, chunks, cut_rows, 0)

    pltpu.make_async_copy(block.at[:others], block.at[:others], field_sem).wait()
    field_hi[...], field_lo[...] = split(block[...])

    rows = 128
    chunks = members // rows
    group = rows // per
    low_bits = lax.rem(me, group)

    def back(k):
        return pltpu.make_async_remote_copy(
            result.at[pl.ds(pl.multiple_of(k * per, per), per), :], out_ref.at[mine],
            send_sem.at[4], back_sem, device_id=place(k), device_id_type=MESH,
        )

    def final_rows(i, carry):
        c = lax.rem(lax.div(me, group) + i, chunks)
        result[at(c), :] = dot3(
            (inv_hi[at(c), :], inv_lo[at(c), :]), (field_hi[...], field_lo[...])
        )

        for j in range(group):
            k = c * group + lax.rem(low_bits + j, group)

            @pl.when(k != me)
            def _(k=k):
                back(k).start()

        return carry

    lax.fori_loop(0, chunks, final_rows, 0)
    out_ref[mine] = result[my_rows, :]

    pltpu.make_async_copy(out_ref.at[: count - 1], out_ref.at[: count - 1], back_sem).wait()
    pltpu.make_async_copy(seen.at[:others], seen.at[:others], send_sem.at[0]).wait()
    pltpu.make_async_copy(block.at[:others], block.at[:others], send_sem.at[1]).wait()
    pltpu.make_async_copy(block.at[:others], block.at[:others], send_sem.at[4]).wait()
    pltpu.make_async_copy(cells.at[: count - 1], cells.at[: count - 1], send_sem.at[5]).wait()


def whole(state, cx, cy, d, index, value, weight):
    per, count, lon = state.shape
    members, width = count * per, value.shape[2]
    tall = count + 2 * FSTEPS
    square = (members, members)
    state, cx, cy, d, index, value, weight = [
        pltpu.with_memory_space_constraint(x, pltpu.HBM)
        for x in (state, cx, cy, d, index, value, weight)
    ]
    return pl.pallas_call(
        whole_kernel,
        out_shape=jax.ShapeDtypeStruct((count, per, lon), F32),
        in_specs=[pl.BlockSpec(memory_space=pltpu.HBM)] * 7,
        out_specs=VMEM,
        scratch_shapes=[pltpu.VMEM((tall, per, lon), F32)] * (FSTEPS + 1)
        + [
            pltpu.VMEM((3, count, lon), F32),
            pltpu.VMEM((5, count, lon), F32),
            pltpu.VMEM((tall, per, lon), F32),
            pltpu.VMEM((count, 1, width), jnp.int32),
            pltpu.VMEM((count, per, width), F32),
            pltpu.VMEM((1, width), F32),
            pltpu.VMEM((3, 1, width), F32),
            pltpu.VMEM((members, lon), F32),
            pltpu.VMEM((members, width), F32),
            pltpu.VMEM((3, members + 8, width), F32),
            pltpu.VMEM((members, lon), F32),
            pltpu.VMEM((members, 1), F32),
            pltpu.VMEM(square, F32),
        ]
        + [pltpu.VMEM(square, BF16)] * 6
        + [pltpu.VMEM((members, 3 * width), BF16)] * 2
        + [pltpu.VMEM((members, lon), BF16)] * 2
        + [
            pltpu.SemaphoreType.DMA,
            pltpu.SemaphoreType.DMA,
            pltpu.SemaphoreType.DMA,
            pltpu.SemaphoreType.DMA((3,)),
            pltpu.SemaphoreType.DMA((8,)),
            pltpu.SemaphoreType.DMA((2, 2)),
            pltpu.SemaphoreType.DMA((2, 2)),
        ]
        + [pltpu.SemaphoreType.DMA] * 8,
        compiler_params=pltpu.CompilerParams(
            collective_id=0, has_side_effects=True, vmem_limit_bytes=42 << 20
        ),
        cost_estimate=pl.CostEstimate(
            flops=10_000_000_000, bytes_accessed=6_000_000, transcendentals=0
        ),
    )(state, cx, cy, d, index, value, weight)


def on_device(starting_states, courant_x, courant_y, diffusion, obs_index, obs_value, loc_weight):
    out = whole(
        starting_states, courant_x, courant_y, diffusion, obs_index, obs_value,
        loc_weight.reshape(3, 1, -1),
    )
    return jnp.transpose(out, (1, 0, 2))


def solution(mesh):
    in_specs = (
        P(("members", "blk"), "lat", None),
        P("lat", None),
        P("lat", None),
        P("lat", None),
        P("lat", ("members", "blk"), None),
        P("lat", ("members", "blk"), None),
        P("lat", ("members", "blk"), None, None),
    )
    out_specs = P(("members", "blk"), "lat", None)
    return jax.shard_map(
        on_device, mesh=mesh, in_specs=in_specs, out_specs=out_specs, check_vma=False
    )
```

```python
import functools

import jax
import jax.numpy as jnp
from jax import lax
from jax.experimental import pallas as pl
from jax.experimental.pallas import tpu as pltpu
from jax.sharding import PartitionSpec as P

FSTEPS = 8
NS_ITERS = 4
ROWS = 16
EARLY = 2
AHEAD = 2
ALONE = 1
SPIRAL = (1, 7, 2, 6, 3, 5, 4, 0)
MESH = pl.DeviceIdType.MESH
VMEM = pl.BlockSpec(memory_space=pltpu.VMEM)
F32 = jnp.float32
BF16 = jnp.bfloat16


def split(x):
    high = x.astype(BF16)
    return high, (x - high.astype(F32)).astype(BF16)


def dot3(a, b, contract=((1,), (0,))):
    def one(p, q):
        return lax.dot_general(p, q, (contract, ((), ())), preferred_element_type=F32)

    return one(a[0], b[0]) + (one(a[0], b[1]) + one(a[1], b[0]))


def whole_kernel(
    state_ref, cx_ref, cy_ref, d_ref, index_ref, value_ref, weight_ref, out_ref,
    l0, l1, l2, l3, l4, l5, l6, l7, l8,
    raw, dense, coef, cells, obs, value, weight, block, seen, stack, result,
    spread_ref, gram, left_hi, left_lo, right_hi, right_lo, inv_hi, inv_lo, wide_hi, wide_lo, field_hi, field_lo,
    load_sem, raw_sem, coef_sem, own_sem, send_sem, edge_send, edge_recv,
    cell_sem, value_sem, weight_sem, obs_sem, field_sem, low_sem, high_sem, back_sem,
):
    levels = (l0, l1, l2, l3, l4, l5, l6, l7, l8)
    per, count, lon = state_ref.shape
    members = count * per
    tall = count + 2 * FSTEPS
    lo = lax.axis_index("members")
    bl = lax.axis_index("blk")
    lat = lax.axis_index("lat")
    n_lat = lax.axis_size("lat")
    n_blk = lax.axis_size("blk")
    me = lo * n_blk + bl
    my_z, my_y, my_core = (lo // 8) * 4 + bl, (lo // 2) % 4, lo % 2

    def set_at(z, y, core):
        return (((z // 4) * 4 + y) * 2 + core) * 4 + z % 4

    def block_at(z, y, core):
        return (z * 4 + y + (z % 2) * (3 - 2 * y)) * 2 + core

    def own_of(b):
        z, y = b // 8, (b // 2) % 4
        return set_at(z, y + (z % 2) * (3 - 2 * y), b % 2)

    def place(k):
        return {"members": k // n_blk, "blk": k % n_blk}

    zs = [lax.rem(my_z + dz, 8) for dz in range(8)]
    z_sets = [lax.div(z, 4) * 8 for z in zs]
    z_blks = [lax.rem(z, 4) for z in zs]

    def each(first, last, act):
        def group(q, carry):
            y = lax.rem(my_y + lax.div(q, 2), 4)
            core = lax.rem(my_core + lax.rem(q, 2), 2)
            even, odd = y * 2 + core, (3 - y) * 2 + core
            for dz in SPIRAL:
                z = zs[dz]
                m, blk = z_sets[dz] + even, z_blks[dz]
                b = z * 8 + even + lax.rem(z, 2) * (odd - even)
                run = functools.partial(act, {"members": m, "blk": blk}, m * 4 + blk, b, z)
                if dz == 0:
                    pl.when(q > 0)(run)
                else:
                    run()
            return carry

        lax.fori_loop(first, last, group, 0)

    mine = block_at(my_z, my_y, my_core)
    my_rows = pl.ds(pl.multiple_of(me * per, per), per)
    inner = pl.ds(FSTEPS, count)

    for i, ref in enumerate((cx_ref, cy_ref, d_ref)):
        pltpu.make_async_copy(ref, raw.at[i], raw_sem).start()
    pltpu.make_async_copy(index_ref.at[0], cells.at[me], own_sem.at[0]).start()
    for m in range(per):
        pltpu.make_async_copy(state_ref.at[m], l0.at[inner, m, :], load_sem).start()

    barrier = pltpu.get_barrier_semaphore()

    @pl.when(lat > 0)
    def _():
        pl.semaphore_signal(barrier, inc=1, device_id={"lat": lat - 1}, device_id_type=MESH)

    @pl.when(lat < n_lat - 1)
    def _():
        pl.semaphore_signal(barrier, inc=1, device_id={"lat": lat + 1}, device_id_type=MESH)

    def greet(device, k, b, z):
        pl.semaphore_signal(barrier, inc=1, device_id=device, device_id_type=MESH)

    each(0, 8, greet)

    pltpu.make_async_copy(raw, raw, raw_sem).wait()
    cx, cy, d = 0.5 * raw[0], 0.5 * raw[1], raw[2]
    for i, term in enumerate((d - cx, d + cx, d - cy, d + cy, 1.0 - 4.0 * d)):
        dense[i] = term
        pltpu.make_async_copy(dense.at[i], coef.at[inner, i, :], coef_sem).start()
    low_rows, high_rows = pl.ds(0, FSTEPS), pl.ds(FSTEPS + count, FSTEPS)

    @pl.when(lat == 0)
    def _():
        l0[low_rows] = jnp.zeros((FSTEPS, per, lon), F32)
        coef[low_rows] = jnp.zeros((FSTEPS, per, lon), F32)

    @pl.when(lat == n_lat - 1)
    def _():
        l0[high_rows] = jnp.zeros((FSTEPS, per, lon), F32)
        coef[high_rows] = jnp.zeros((FSTEPS, per, lon), F32)

    lane = lax.broadcasted_iota(jnp.int32, (per, 128), 1)
    parts = lon // 128

    def advance_row(step, r):
        old, new = levels[step - 1], levels[step]
        pieces = [old[r, :, p * 128 : (p + 1) * 128] for p in range(parts)]
        right = [pltpu.roll(v, 1, 1) for v in pieces]
        left = [pltpu.roll(v, 127, 1) for v in pieces]
        for p in range(parts):
            here = slice(p * 128, (p + 1) * 128)
            west = jnp.where(lane == 0, right[p - 1], right[p])
            east = jnp.where(lane == 127, left[(p + 1) % parts], left[p])
            c = [jnp.broadcast_to(coef[r, pl.ds(i, 1), here], lane.shape) for i in range(5)]
            new[r, :, here] = (
                (c[4] * pieces[p] + c[0] * east)
                + (c[1] * west + c[2] * old[r + 1, :, here])
                + c[3] * old[r - 1, :, here]
            )

    def inner_step(step):
        low, high = FSTEPS + step, FSTEPS + count - step

        def rows(i, carry):
            start = jnp.minimum(low + ROWS * i, high - ROWS)
            for u in range(ROWS):
                advance_row(step, start + u)
            return carry

        lax.fori_loop(0, (high - low + ROWS - 1) // ROWS, rows, 0)

    pltpu.make_async_copy(l0.at[inner], l0.at[inner], load_sem).wait()
    pltpu.make_async_copy(dense, dense, coef_sem).wait()
    for step in range(1, ALONE + 1):
        inner_step(step)
    pl.semaphore_wait(
        barrier, count - 1 + jnp.where(lat > 0, 1, 0) + jnp.where(lat < n_lat - 1, 1, 0)
    )

    def edges(up):
        source = pl.ds(count if up else FSTEPS, FSTEPS)
        target = low_rows if up else high_rows
        side = 0 if up else 1
        device = {"lat": lat + 1 if up else lat - 1}
        return [
            pltpu.make_async_remote_copy(
                l0.at[source], l0.at[target], edge_send.at[side, 0], edge_recv.at[side, 0],
                device_id=device, device_id_type=MESH,
            ),
            pltpu.make_async_remote_copy(
                coef.at[source, 0:3, :], coef.at[target, 0:3, :], edge_send.at[side, 1],
                edge_recv.at[side, 1], device_id=device, device_id_type=MESH,
            ),
        ]

    def send_cells(device, k, b, z):
        pltpu.make_async_remote_copy(
            index_ref.at[0], cells.at[me], send_sem.at[5], cell_sem,
            device_id=device, device_id_type=MESH,
        ).start()

    each(0, 8, send_cells)

    @pl.when(lat < n_lat - 1)
    def _():
        for copy in edges(True):
            copy.start()

    @pl.when(lat > 0)
    def _():
        for copy in edges(False):
            copy.start()


    def send_terms():
        owner = place(own_of(me))
        return [
            pltpu.make_async_remote_copy(
                value_ref.at[0], value, send_sem.at[6], value_sem,
                device_id=owner, device_id_type=MESH,
            ),
            pltpu.make_async_remote_copy(
                weight_ref, weight, send_sem.at[7], weight_sem,
                device_id=owner, device_id_type=MESH,
            ),
        ]

    def keep_terms():
        return [
            pltpu.make_async_copy(value_ref.at[0], value, own_sem.at[1]),
            pltpu.make_async_copy(weight_ref, weight, own_sem.at[2]),
        ]

    @pl.when(mine == me)
    def _():
        for copy in keep_terms():
            copy.start()

    @pl.when(mine != me)
    def _():
        for copy in send_terms():
            copy.start()

    for step in range(ALONE + 1, FSTEPS + 1):
        inner_step(step)

    def send_field(device, k, b, z):
        pltpu.make_async_remote_copy(
            l8.at[FSTEPS + b], block.at[my_rows, :], send_sem.at[1], field_sem,
            device_id=device, device_id_type=MESH,
        ).start()

    def away_from_edge(z):
        return (z > 0) & (z < 7)

    def send_early(device, k, b, z):
        pl.when(away_from_edge(z))(functools.partial(send_field, device, k, b, z))

    def send_late(device, k, b, z):
        pl.when(jnp.logical_not(away_from_edge(z)))(functools.partial(send_field, device, k, b, z))

    pltpu.make_async_copy(cells.at[: count - 1], cells.at[: count - 1], cell_sem).wait()
    pltpu.make_async_copy(index_ref.at[0], cells.at[me], own_sem.at[0]).wait()

    def observe(i, carry):
        for u in range(8):
            b = i * 8 + u
            index = jnp.broadcast_to(cells[b], lane.shape)
            where, group = jnp.bitwise_and(index, 127), jnp.right_shift(index, 7)
            found = jnp.zeros(lane.shape, F32)
            for p in range(parts):
                picked = jnp.take_along_axis(
                    l8[FSTEPS + b, :, p * 128 : (p + 1) * 128], where, axis=1
                )
                found = jnp.where(group == p, picked, found)
            obs[b] = found
        return carry

    lax.fori_loop(1, count // 8 - 1, observe, 0)

    def send_obs(device, k, b, z):
        pltpu.make_async_remote_copy(
            obs.at[b], seen.at[my_rows, :], send_sem.at[0], obs_sem,
            device_id=device, device_id_type=MESH,
        ).start()

    def send_inner_obs(device, k, b, z):
        pl.when(away_from_edge(z))(functools.partial(send_obs, device, k, b, z))

    def send_edge_obs(device, k, b, z):
        pl.when(jnp.logical_not(away_from_edge(z)))(functools.partial(send_obs, device, k, b, z))

    each(0, 8, send_inner_obs)
    each(1, 1 + EARLY, send_early)

    @pl.when(lat > 0)
    def _():
        for copy in edges(True):
            copy.wait_recv()
        for copy in edges(False):
            copy.wait_send()

    @pl.when(lat < n_lat - 1)
    def _():
        for copy in edges(False):
            copy.wait_recv()
        for copy in edges(True):
            copy.wait_send()

    for edge in (low_rows, high_rows):
        twice = coef[edge, 0:1, :] + coef[edge, 1:2, :]
        coef[edge, 3:4, :] = twice - coef[edge, 2:3, :]
        coef[edge, 4:5, :] = 1.0 - 2.0 * twice

    for step in range(1, FSTEPS + 1):
        for u in range(FSTEPS):
            advance_row(step, step + u)
            advance_row(step, tall - step - FSTEPS + u)

    lax.fori_loop(0, 1, observe, 0)
    lax.fori_loop(count // 8 - 1, count // 8, observe, 0)

    each(0, 8, send_edge_obs)
    each(1, 1 + EARLY, send_late)
    each(1 + EARLY, 1 + AHEAD, send_field)
    seen[my_rows, :] = obs[mine]
    block[my_rows, :] = l8[FSTEPS + mine]

    @pl.when(mine != me)
    def _():
        for copy in send_terms():
            copy.wait()

    @pl.when(mine == me)
    def _():
        for copy in keep_terms():
            copy.wait()

    others = (count - 1) * per
    pltpu.make_async_copy(seen.at[:others], seen.at[:others], obs_sem).wait()

    ybar = jnp.mean(seen[...], axis=0, keepdims=True)
    own = seen[...] - ybar
    stack[1, :members, :] = own
    stack[1, members:, :] = jnp.broadcast_to(value[...] - ybar, (8, own.shape[1]))

    def to_low():
        return pltpu.make_async_remote_copy(
            stack.at[1], stack.at[2], send_sem.at[2], high_sem,
            device_id=place(own_of(mine - 1)), device_id_type=MESH,
        )

    def to_high():
        return pltpu.make_async_remote_copy(
            stack.at[1], stack.at[0], send_sem.at[3], low_sem,
            device_id=place(own_of(mine + 1)), device_id_type=MESH,
        )

    @pl.when(mine > 0)
    def _():
        to_low().start()

    @pl.when(mine < count - 1)
    def _():
        to_high().start()

    each(1 + AHEAD, 8, send_field)
    each(0, 1, send_field)

    @pl.when(mine == 0)
    def _():
        stack[0] = jnp.zeros(stack.shape[1:], F32)

    @pl.when(mine == count - 1)
    def _():
        stack[2] = jnp.zeros(stack.shape[1:], F32)

    @pl.when(mine > 0)
    def _():
        to_low().wait_send()
        to_high().wait_recv()

    @pl.when(mine < count - 1)
    def _():
        to_high().wait_send()
        to_low().wait_recv()

    obs = own.shape[1]
    pull_row = jnp.zeros((1, members), F32)
    for part in range(3):
        held = stack[part, :members, :]
        weighted = held * weight[part]
        pull_row = pull_row + lax.dot_general(
            stack[part, pl.ds(members, 8), :], weighted, (((1,), (1,)), ((), ())),
            precision=lax.Precision.HIGHEST, preferred_element_type=F32,
        )[0:1]
        here = slice(part * obs, (part + 1) * obs)
        wide_hi[:, here], wide_lo[:, here] = split(held)
        left_hi[:, here], left_lo[:, here] = split(weighted)

    rows = 256
    chunks = members // rows

    def eye(start):
        row = lax.broadcasted_iota(jnp.int32, (rows, members), 0) + start
        return (row == lax.broadcasted_iota(jnp.int32, (rows, members), 1)).astype(F32)

    def at(i):
        return pl.ds(pl.multiple_of(i * rows, rows), rows)

    width = 3 * obs

    def gram_rows(i, total):
        part = dot3(
            (left_hi[at(i), :width], left_lo[at(i), :width]),
            (wide_hi[...], wide_lo[...]), ((1,), (1,)),
        )
        part = part / (members - 1) + eye(i * rows)
        gram[at(i), :] = part
        return total + jnp.sum(part * part, keepdims=True)

    total = lax.fori_loop(0, chunks, gram_rows, jnp.zeros((1, 1), F32))
    frobenius = jnp.sqrt(total + 1e-06)

    def scale_rows(i, carry):
        gram[at(i), :] = gram[at(i), :] / frobenius
        return carry

    lax.fori_loop(0, chunks, scale_rows, 0)

    for repeat in range(NS_ITERS):
        last = repeat == NS_ITERS - 1

        def factor_rows(i, carry, repeat=repeat):
            now = gram[at(i), :]
            right_hi[at(i), :], right_lo[at(i), :] = split(1.5 * eye(i * rows) - 0.5 * now)
            left_hi[at(i), :], left_lo[at(i), :] = split(now)
            if repeat == 0:
                inv_hi[at(i), :], inv_lo[at(i), :] = right_hi[at(i), :], right_lo[at(i), :]
            return carry

        lax.fori_loop(0, chunks, factor_rows, 0)

        def step_rows(i, carry, repeat=repeat, last=last):
            right = (right_hi[...], right_lo[...])
            if not last:
                half = dot3((left_hi[at(i), :], left_lo[at(i), :]), right)
                gram[at(i), :] = dot3(split(half), right)
            if repeat > 0:
                inverse = dot3((inv_hi[at(i), :], inv_lo[at(i), :]), right)
                if last:
                    gram[at(i), :] = inverse / jnp.sqrt(frobenius)
                else:
                    inv_hi[at(i), :], inv_lo[at(i), :] = split(inverse)
            return carry

        lax.fori_loop(0, chunks, step_rows, 0)

    inner = jnp.sum(gram[...] * pull_row, axis=1, keepdims=True)
    shift = jnp.sum(gram[...] * inner, axis=0, keepdims=True) / (members - 1)

    spread = 1.0 - jnp.sum(gram[...], axis=1, keepdims=True) - jnp.sum(shift, keepdims=True)
    spread_ref[...] = spread / members

    def cut_rows(i, carry):
        inv_hi[at(i), :], inv_lo[at(i), :] = split(
            gram[at(i), :] + shift + spread_ref[at(i), :]
        )
        return carry

    lax.fori_loop(0, chunks, cut_rows, 0)

    pltpu.make_async_copy(block.at[:others], block.at[:others], field_sem).wait()
    field_hi[...], field_lo[...] = split(block[...])

    rows = 128
    chunks = members // rows
    group = rows // per
    low_bits = lax.rem(me, group)

    def back(k):
        return pltpu.make_async_remote_copy(
            result.at[pl.ds(pl.multiple_of(k * per, per), per), :], out_ref.at[mine],
            send_sem.at[4], back_sem, device_id=place(k), device_id_type=MESH,
        )

    def final_rows(i, carry):
        c = lax.rem(lax.div(me, group) + i, chunks)
        result[at(c), :] = dot3(
            (inv_hi[at(c), :], inv_lo[at(c), :]), (field_hi[...], field_lo[...])
        )

        for j in range(group):
            k = c * group + lax.rem(low_bits + j, group)

            @pl.when(k != me)
            def _(k=k):
                back(k).start()

        return carry

    lax.fori_loop(0, chunks, final_rows, 0)
    out_ref[mine] = result[my_rows, :]

    pltpu.make_async_copy(out_ref.at[: count - 1], out_ref.at[: count - 1], back_sem).wait()
    pltpu.make_async_copy(seen.at[:others], seen.at[:others], send_sem.at[0]).wait()
    pltpu.make_async_copy(block.at[:others], block.at[:others], send_sem.at[1]).wait()
    pltpu.make_async_copy(block.at[:others], block.at[:others], send_sem.at[4]).wait()
    pltpu.make_async_copy(cells.at[: count - 1], cells.at[: count - 1], send_sem.at[5]).wait()


def whole(state, cx, cy, d, index, value, weight):
    per, count, lon = state.shape
    members, width = count * per, value.shape[2]
    tall = count + 2 * FSTEPS
    square = (members, members)
    state, cx, cy, d, index, value, weight = [
        pltpu.with_memory_space_constraint(x, pltpu.HBM)
        for x in (state, cx, cy, d, index, value, weight)
    ]
    return pl.pallas_call(
        whole_kernel,
        out_shape=jax.ShapeDtypeStruct((count, per, lon), F32),
        in_specs=[pl.BlockSpec(memory_space=pltpu.HBM)] * 7,
        out_specs=VMEM,
        scratch_shapes=[pltpu.VMEM((tall, per, lon), F32)] * (FSTEPS + 1)
        + [
            pltpu.VMEM((3, count, lon), F32),
            pltpu.VMEM((5, count, lon), F32),
            pltpu.VMEM((tall, per, lon), F32),
            pltpu.VMEM((count, 1, width), jnp.int32),
            pltpu.VMEM((count, per, width), F32),
            pltpu.VMEM((1, width), F32),
            pltpu.VMEM((3, 1, width), F32),
            pltpu.VMEM((members, lon), F32),
            pltpu.VMEM((members, width), F32),
            pltpu.VMEM((3, members + 8, width), F32),
            pltpu.VMEM((members, lon), F32),
            pltpu.VMEM((members, 1), F32),
            pltpu.VMEM(square, F32),
        ]
        + [pltpu.VMEM(square, BF16)] * 6
        + [pltpu.VMEM((members, 3 * width), BF16)] * 2
        + [pltpu.VMEM((members, lon), BF16)] * 2
        + [
            pltpu.SemaphoreType.DMA,
            pltpu.SemaphoreType.DMA,
            pltpu.SemaphoreType.DMA,
            pltpu.SemaphoreType.DMA((3,)),
            pltpu.SemaphoreType.DMA((8,)),
            pltpu.SemaphoreType.DMA((2, 2)),
            pltpu.SemaphoreType.DMA((2, 2)),
        ]
        + [pltpu.SemaphoreType.DMA] * 8,
        compiler_params=pltpu.CompilerParams(
            collective_id=0, has_side_effects=True, vmem_limit_bytes=42 << 20
        ),
        cost_estimate=pl.CostEstimate(
            flops=10_000_000_000, bytes_accessed=6_000_000, transcendentals=0
        ),
    )(state, cx, cy, d, index, value, weight)


def on_device(starting_states, courant_x, courant_y, diffusion, obs_index, obs_value, loc_weight):
    out = whole(
        starting_states, courant_x, courant_y, diffusion, obs_index, obs_value,
        loc_weight.reshape(3, 1, -1),
    )
    return jnp.transpose(out, (1, 0, 2))


def solution(mesh):
    in_specs = (
        P(("members", "blk"), "lat", None),
        P("lat", None),
        P("lat", None),
        P("lat", None),
        P("lat", ("members", "blk"), None),
        P("lat", ("members", "blk"), None),
        P("lat", ("members", "blk"), None, None),
    )
    out_specs = P(("members", "blk"), "lat", None)
    return jax.shard_map(
        on_device, mesh=mesh, in_specs=in_specs, out_specs=out_specs, check_vma=False
    )
```
